128 devices in a mesh: row: 8 (over z, core), col: 16 (over y, x).
Axes of the slice: x: 4, y: 4, z: 4, core: 2. Of those that a mesh axis runs over, the one named last changes fastest.
Arguments:
- panel_block: float32 [512, 512], P(('row', 'col')), may hold values from -1 to 10, as said below
- panel_cross: float32 [8192, 512], P('col'), may hold values from -0.375 to 0.375
- trail_block: float32 [8192, 8192], P('row', 'col'), may hold values from -1.2 to 1.2
- panel_pixels: float32 [512, 32768], P('row', 'col'), may hold values from -0.375 to 0.375
- trail_pixels: float32 [8192, 32768], P('row', 'col'), may hold values from -1.2 to 1.2
- panel_sectors: float32 [512, 1024], P('row'), may hold values from -6 to 6
- trail_sectors: float32 [8192, 1024], P('col', 'row'), may hold values from -1.2 to 1.2
Outputs:
- panel_factor: float32 [512, 512], P(('row', 'col'))
- panel_columns: float32 [8192, 512], P('col')
- trail_updated: float32 [8192, 8192], P('row', 'col')
- pixels_updated: float32 [8192, 32768], P('row', 'col')
- sectors_updated: float32 [8192, 1024], P('col', 'row')
- prediction: float32 [32768, 1024], P('col', 'row')
The draws below stay inside these ranges and needn't reach their ends.
Inputs may be any that keep to these rules, and one draw needn't show every extreme that they name: `panel_block`: symmetric positive definite.
All inputs are finite; a program needn't handle non-finite values.
Results may differ from the reference program's by a relative error of at most 0.000075.
Values sent between devices are 32-bit elements; how exact they have to be, the bound alone decides.
A program may use at most 128 MiB of HBM per device.

```python
import jax
import jax.numpy as jnp
from jax import lax

PANEL = 256
PW = 512
TRAIL = 8192
PIXELS = 32768
SECTORS = 1024


def draw_panel_block(key, part):
    first_key, second_key = jax.random.split(jax.random.fold_in(key, 11))
    raw = jax.random.normal(first_key, (PW, PW), jnp.float32)
    scales = jnp.exp(jax.random.uniform(second_key, (PW,), jnp.float32, 0.0, 1.3862944))
    product = jnp.dot(raw, raw.T, precision=lax.Precision.HIGHEST)
    return 0.5 * product / PW + jnp.diag(scales)


def steps_of(own_key, extent, cuts, least, top_value):
    gain = 1.0
    for dim, blocks in cuts:
        heights = jax.random.uniform(jax.random.fold_in(jax.random.fold_in(own_key, 6), dim), (blocks,), jnp.float32, least / len(cuts), top_value / len(cuts))
        gain = gain * jnp.repeat(jnp.exp(heights), extent[dim] // blocks).reshape((-1,) + (1,) * (len(extent) - 1 - dim))
    return gain


def normal_values(rng, extent, scale, limit, pieces=(), held_as=jnp.bfloat16):
    result = scale * jax.random.normal(rng, extent, jnp.float32)
    if pieces:
        result = result * steps_of(rng, extent, pieces, -0.22, 0.18)
    return jnp.clip(result, -limit, limit).astype(held_as)


def setup_inputs(seed: int = 0) -> dict:
    streams_of = jax.random.split(jax.random.key(seed), 8)
    return {
        "panel_block": draw_panel_block(jax.random.fold_in(streams_of[7], 71), 0),
        "panel_cross": normal_values(streams_of[1], (TRAIL, PW), PANEL ** -0.5, 0.375, ((0, 16),), jnp.float32),
        "trail_block": normal_values(streams_of[2], (TRAIL, TRAIL), 0.2, 1.2, ((0, 8), (1, 16)), jnp.float32),
        "panel_pixels": normal_values(streams_of[3], (PW, PIXELS), PANEL ** -0.5, 0.375, ((0, 8), (1, 16)), jnp.float32),
        "trail_pixels": normal_values(streams_of[4], (TRAIL, PIXELS), 0.2, 1.2, ((0, 8), (1, 16)), jnp.float32),
        "panel_sectors": normal_values(streams_of[5], (PW, SECTORS), 1.0, 6.0, ((0, 8),), jnp.float32),
        "trail_sectors": normal_values(streams_of[6], (TRAIL, SECTORS), 0.2, 1.2, ((0, 16), (1, 8)), jnp.float32),
    }


def reference(panel_block, panel_cross, trail_block, panel_pixels, trail_pixels, panel_sectors, trail_sectors):
    highest = lax.Precision.HIGHEST
    factor = jnp.linalg.cholesky(panel_block)
    columns = lax.linalg.triangular_solve(factor, panel_cross, left_side=False, lower=True, transpose_a=True)
    trail_updated = trail_block - lax.dot_general(columns, columns, (((1,), (1,)), ((), ())), precision=highest)
    solved = lax.linalg.triangular_solve(factor, panel_sectors, left_side=True, lower=True)
    kriging_weights = lax.linalg.triangular_solve(factor, solved, left_side=True, lower=True, transpose_a=True)
    sectors_updated = trail_sectors - jnp.dot(columns, solved, precision=highest)
    coupling = lax.linalg.triangular_solve(factor, columns, left_side=False, lower=True)
    pixels_updated = trail_pixels - jnp.dot(coupling, panel_pixels, precision=highest)
    prediction = lax.dot_general(panel_pixels, kriging_weights, (((0,), (0,)), ((), ())), precision=highest)
    return (factor, columns, trail_updated, pixels_updated, sectors_updated, prediction)
```

```python
import functools

import jax
import jax.numpy as jnp
from jax import lax
from jax.experimental import pallas as pl
from jax.experimental.pallas import tpu as pltpu
from jax.sharding import PartitionSpec as P

HIGHEST = lax.Precision.HIGHEST
HIGH = lax.Precision.HIGH
MESH = pl.DeviceIdType.MESH
TILE = (8, 128)


def gather_kernel(own_ref, all_ref, send_sem, recv_sem):
    row, col = lax.axis_index("row"), lax.axis_index("col")
    z, core = row // 2, lax.rem(row, 2)
    y, x = col // 4, lax.rem(col, 4)
    turn = lambda value, k: lax.rem(value + k, 4)
    twin = (z * 2 + 1 - core, col)
    x_peer = [(row, y * 4 + turn(x, k)) for k in (1, 2, 3)]
    y_peer = [(row, turn(y, k) * 4 + x) for k in (1, 2, 3)]
    z_peer = [(turn(z, k) * 2 + core, col) for k in (1, 2, 3)]

    barrier = pltpu.get_barrier_semaphore()
    for peer in x_peer + y_peer + z_peer + [twin]:
        pl.semaphore_signal(barrier, inc=1, device_id=peer, device_id_type=MESH)
    me = row * 16 + col
    all_ref[pl.ds(me, 1)] = own_ref[...]
    pl.semaphore_wait(barrier, 10)

    sent = []

    def send(start, count, peer, slot):
        part = all_ref.at[pl.ds(start, count)]
        copy = pltpu.make_async_remote_copy(
            src_ref=part,
            dst_ref=part,
            send_sem=send_sem.at[slot],
            recv_sem=recv_sem.at[slot],
            device_id=peer,
            device_id_type=MESH,
        )
        copy.start()
        sent.append(copy)

    def arrive(start, count, slot):
        part = all_ref.at[pl.ds(start, count)]
        pltpu.make_async_copy(part, part, recv_sem.at[slot]).wait()

    for k in range(3):
        send(me, 1, x_peer[k], k)
    for k in range(3):
        arrive(row * 16 + y * 4 + turn(x, 3 - k), 1, k)
    for k in range(3):
        send(row * 16 + y * 4, 4, y_peer[k], 3 + k)
    for k in range(3):
        arrive(row * 16 + turn(y, 3 - k) * 4, 4, 3 + k)
    for k in range(3):
        send(row * 16, 16, z_peer[k], 6 + k)
    send(row * 16, 16, twin, 9)
    for k in range(3):
        source = turn(z, 3 - k)
        arrive(source * 32 + core * 16, 16, 6 + k)
        send(source * 32 + core * 16, 16, twin, 10 + k)
    arrive(z * 32 + (1 - core) * 16, 16, 9)
    for k in range(3):
        arrive(turn(z, 3 - k) * 32 + (1 - core) * 16, 16, 10 + k)
    for copy in sent:
        copy.wait_send()


def gather_block(own):
    return pl.pallas_call(
        gather_kernel,
        out_shape=jax.ShapeDtypeStruct((128, 4, 512), jnp.float32),
        in_specs=[pl.BlockSpec(memory_space=pltpu.VMEM)],
        out_specs=pl.BlockSpec(memory_space=pltpu.VMEM),
        scratch_shapes=[pltpu.SemaphoreType.DMA((13,)), pltpu.SemaphoreType.DMA((13,))],
        compiler_params=pltpu.CompilerParams(collective_id=0, has_side_effects=True),
        name="gather_block",
    )(own.reshape(1, 4, 512))


def dot_nn(a, b):
    return lax.dot_general(
        a, b, (((1,), (0,)), ((), ())), precision=HIGHEST, preferred_element_type=jnp.float32
    )


def dot_nt(a, b):
    return lax.dot_general(
        a, b, (((1,), (1,)), ((), ())), precision=HIGHEST, preferred_element_type=jnp.float32
    )


def invert_tile(load, store):
    lane = lax.broadcasted_iota(jnp.int32, TILE, 1)
    sub = lax.broadcasted_iota(jnp.int32, TILE, 0)
    here = [sub == j for j in range(8)]

    def lanes(x, k):
        return jnp.broadcast_to(x[:, k : k + 1], TILE)

    def rows(x, j):
        return jnp.broadcast_to(x[j : j + 1, :], TILE)

    block = [load(i) for i in range(16)]
    for g in range(16):
        first = 8 * g
        in_group = (lane >= first) & (lane < first + 8)
        pivot = [lanes(block[g], first + k) for k in range(8)]
        rest = jnp.where(in_group, jnp.where(lane - first == sub, 1.0, 0.0), block[g])
        inverse = jnp.zeros(TILE, jnp.float32)
        for j in range(8):
            row = rows(rest, j)
            entry = {k: rows(pivot[k], j) for k in range(j, 8)}
            recip = 1.0 / entry[j]
            inverse = jnp.where(here[j], row * lax.rsqrt(entry[j]), inverse)
            factor = jnp.where(here[j], -recip, pivot[j] * recip)
            rest = jnp.where(here[j], 0.0, rest) - factor * row
            for k in range(j + 1, 8):
                pivot[k] = jnp.where(here[j], 0.0, pivot[k]) - factor * entry[k]
        store(g, jnp.where(lane < first + 8, inverse, 0.0))
        if g < 15:
            spread = [rows(rest, k) for k in range(8)]
            for i in range(g + 1, 16):
                value = jnp.where(in_group, 0.0, block[i])
                for k in range(8):
                    value = value - lanes(block[i], first + k) * spread[k]
                block[i] = value


def inverse_kernel(a_ref, o_ref, m_ref):
    n = o_ref.shape[0]
    for i in range(n // 4):
        m_ref[4 * i : 4 * i + 4, :] = a_ref[i]
    o_ref[...] = jnp.zeros_like(o_ref)
    for b in range(n // 128):
        s, e = b * 128, b * 128 + 128
        invert_tile(
            lambda i: m_ref[s + 8 * i : s + 8 * i + 8, s:e],
            lambda i, v: o_ref.__setitem__((slice(s + 8 * i, s + 8 * i + 8), slice(s, e)), v),
        )
        inverse = o_ref[s:e, s:e]
        if b:
            o_ref[s:e, :s] = dot_nn(inverse, m_ref[s:e, :s])
        if e < n:
            below = dot_nt(m_ref[e:, s:e], inverse)
            m_ref[e:, e:] -= dot_nt(below, below)
            if b:
                m_ref[e:, :s] -= dot_nn(below, o_ref[s:e, :s])
            m_ref[e:, s:e] = -dot_nn(below, inverse)


def inverse_factor(a):
    n = a.shape[2]
    return pl.pallas_call(
        inverse_kernel,
        out_shape=jax.ShapeDtypeStruct((n, n), jnp.float32),
        in_specs=[pl.BlockSpec(memory_space=pltpu.VMEM)],
        out_specs=pl.BlockSpec(memory_space=pltpu.VMEM),
        scratch_shapes=[pltpu.VMEM((n, n), jnp.float32)],
        compiler_params=pltpu.CompilerParams(vmem_limit_bytes=32 << 20),
        cost_estimate=pl.CostEstimate(flops=60_000_000_000, bytes_accessed=3 << 20, transcendentals=0),
        name="inverse_factor",
    )(a)


def shards(
    panel_block, panel_cross, trail_block, panel_pixels, trail_pixels, panel_sectors, trail_sectors
):
    row_index = lax.axis_index("row")
    col_index = lax.axis_index("col")
    rows_piece = lax.all_gather(panel_pixels, "row", axis=0, tiled=True)
    sectors_full = lax.all_gather(panel_sectors, "row", axis=0, tiled=True)
    pieces = []
    for s in range(2):
        perm = [
            (r * 16 + c, (c // 2) * 16 + 2 * r + (c + s) % 2) for r in range(8) for c in range(16)
        ]
        pieces.append(lax.ppermute(panel_cross, ("row", "col"), perm))
    odd = lax.rem(col_index, 2) == 1
    cross_rows = jnp.concatenate(
        [jnp.where(odd, pieces[1], pieces[0]), jnp.where(odd, pieces[0], pieces[1])], axis=0
    )
    block = gather_block(panel_block)
    inverse = inverse_factor(block)

    def dot(a, b, ca, cb):
        return lax.dot_general(a, b, (((ca,), (cb,)), ((), ())), precision=HIGH)

    n = inverse.shape[0]
    device_index = row_index * lax.axis_size("col") + col_index
    factor_rows = lax.dot_general(
        panel_block, inverse, (((1,), (1,)), ((), ())), precision=HIGHEST
    )
    own_row = device_index * 4 + lax.broadcasted_iota(jnp.int32, (4, n), 0)
    factor_rows = jnp.where(lax.broadcasted_iota(jnp.int32, (4, n), 1) <= own_row, factor_rows, 0.0)
    column_own = dot(panel_cross, inverse, 1, 1)
    row_block = dot(cross_rows, inverse, 1, 1)
    trail_updated = trail_block - dot(row_block, column_own, 1, 1)
    coupling = dot(row_block, inverse, 1, 0)
    pixel_total = trail_pixels - dot(coupling, rows_piece, 1, 0)
    width = trail_sectors.shape[1]
    sector_block = lax.dynamic_slice_in_dim(sectors_full, row_index * width, width, 1)
    solved = dot(inverse, sector_block, 1, 0)
    kriging_weights = dot(inverse, solved, 0, 0)
    sectors_updated = trail_sectors - dot(column_own, solved, 1, 0)
    predicted = dot(rows_piece, kriging_weights, 0, 0)
    return (factor_rows, column_own, trail_updated, pixel_total, sectors_updated, predicted)


def solution(mesh):
    return jax.shard_map(
        shards,
        mesh=mesh,
        in_specs=(
            P(("row", "col"), None),
            P("col", None),
            P("row", "col"),
            P("row", "col"),
            P("row", "col"),
            P("row", None),
            P("col", "row"),
        ),
        out_specs=(
            P(("row", "col"), None),
            P("col", None),
            P("row", "col"),
            P("row", "col"),
            P("col", "row"),
            P("col", "row"),
        ),
        check_vma=False,
    )
```

```python
import functools

import jax
import jax.numpy as jnp
from jax import lax
from jax.experimental import pallas as pl
from jax.experimental.pallas import tpu as pltpu
from jax.sharding import PartitionSpec as P

HIGHEST = lax.Precision.HIGHEST
MESH = pl.DeviceIdType.MESH
TILE = (8, 128)
CHUNKS = 4


def dot_nn(a, b):
    return lax.dot_general(
        a, b, (((1,), (0,)), ((), ())), precision=HIGHEST, preferred_element_type=jnp.float32
    )


def dot_nt(a, b):
    return lax.dot_general(
        a, b, (((1,), (1,)), ((), ())), precision=HIGHEST, preferred_element_type=jnp.float32
    )


def invert_tile(block, store, after):
    lane = lax.broadcasted_iota(jnp.int32, TILE, 1)
    sub = lax.broadcasted_iota(jnp.int32, TILE, 0)
    here = [sub == j for j in range(8)]
    zero = jnp.zeros(TILE, jnp.float32)
    lane_all = lax.broadcasted_iota(jnp.int32, (128, 128), 1)

    for g in range(16):
        first = 8 * g
        top = block[:8]
        in_group = (lane >= first) & (lane < first + 8)
        unit = (lane - first == sub).astype(jnp.float32)
        pivot = [jnp.broadcast_to(top[:, first + k : first + k + 1], TILE) for k in range(8)]
        rest = lax.select(in_group, unit, top)
        inverse = zero
        for j in range(8):
            row = jnp.broadcast_to(rest[j : j + 1], TILE)
            entry = {k: jnp.broadcast_to(pivot[k][j : j + 1], TILE) for k in range(j, 8)}
            recip = 1.0 / entry[j]
            inverse = lax.select(here[j], row * lax.rsqrt(entry[j]), inverse)
            factor = lax.select(here[j], -recip, pivot[j] * recip)
            rest = lax.select(here[j], zero, rest) - factor * row
            for k in range(j + 1, 8):
                pivot[k] = lax.select(here[j], zero, pivot[k]) - factor * entry[k]
        store(g, lax.select(lane < first + 8, inverse, zero))
        if g < 15:
            below = block[8:]
            shape = below.shape
            lane_b = lane_all[: shape[0]]
            value = lax.select(
                (lane_b >= first) & (lane_b < first + 8), jnp.zeros(shape, jnp.float32), below
            )
            for k in range(8):
                value = value - jnp.broadcast_to(
                    below[:, first + k : first + k + 1], shape
                ) * jnp.broadcast_to(rest[k : k + 1], shape)
            block = value
        after(g)


def panel_kernel(
    own_ref, cross_ref, pixel_ref, sector_ref,
    inverse_ref, rows_ref, pixels_ref, sectors_ref,
    all_ref, m_ref, block_send, block_recv, cross_send, cross_recv, pixel_send, pixel_recv,
    sector_send, sector_recv, local_sem,
):
    row, col = lax.axis_index("row"), lax.axis_index("col")
    z, core = row // 2, lax.rem(row, 2)
    y, x = col // 4, lax.rem(col, 4)

    def turn(value, k):
        return lax.rem(value + k, 4)

    twin = (z * 2 + 1 - core, col)
    plane = [(row, turn(y, k // 4) * 4 + turn(x, k % 4)) for k in range(1, 16)]
    z_peer = [None] + [(turn(z, k) * 2 + core, col) for k in (1, 2, 3)]
    other_z = [None] + [(turn(z, k) * 2 + 1 - core, col) for k in (1, 2, 3)]
    x_peer = [None] + [(row, y * 4 + turn(x, k)) for k in (1, 2, 3)]
    y_peer = [None] + [(row, turn(y, k) * 4 + x) for k in (1, 2, 3)]

    barrier = pltpu.get_barrier_semaphore()
    partners = plane + z_peer[1:] + other_z[1:] + [twin]
    for peer in partners:
        pl.semaphore_signal(barrier, inc=1, device_id=peer, device_id_type=MESH)
    me = row * 16 + col
    all_ref[pl.ds(me, 1)] = own_ref[...]
    pl.semaphore_wait(barrier, len(partners))

    sent = []

    def send(src, dst, send_sem, recv_sem, peer, keep=True):
        copy = pltpu.make_async_remote_copy(
            src_ref=src, dst_ref=dst, send_sem=send_sem, recv_sem=recv_sem,
            device_id=peer, device_id_type=MESH,
        )
        copy.start()
        if keep:
            sent.append(copy)
        return copy

    def arrive(ref, sem):
        pltpu.make_async_copy(ref, ref, sem).wait()

    for k in range(1, 16):
        part = all_ref.at[pl.ds(me, 1)]
        send(part, part, block_send.at[k - 1], block_recv.at[k - 1], plane[k - 1])

    half = 256
    step = half // CHUNKS

    def slot(which, holder):
        same = 1 - jnp.abs(which // 2 - holder)
        odd = lax.rem(which, 2)
        return same * (2 * odd + holder) + (1 - same) * (4 + odd)

    holds = y == z
    my_slot = slot(x, core)

    def cross_part(q):
        return cross_ref.at[pl.ds(core * half + q * step, step)]

    def rows_part(s, q):
        return rows_ref.at[s, pl.ds(q * step, step)]

    def y_copy(q, k):
        return pltpu.make_async_remote_copy(
            src_ref=cross_part(q), dst_ref=rows_part(my_slot, q),
            send_sem=cross_send.at[0, q, k - 1], recv_sem=cross_recv.at[0, q],
            device_id=y_peer[k], device_id_type=MESH,
        )

    def own_copy(q):
        return pltpu.make_async_copy(cross_part(q), rows_part(my_slot, q), cross_recv.at[0, q])

    @pl.when(holds)
    def _():
        for q in range(CHUNKS):
            own_copy(q).start()
        for q in range(CHUNKS):
            for k in (1, 3, 2):
                y_copy(q, k).start()

    def pass_x(q):
        arrive(rows_part(my_slot, q), cross_recv.at[0, q])
        for i, k in enumerate((1, 3)):
            send(rows_part(my_slot, q), rows_part(my_slot, q),
                 cross_send.at[1, q, i], cross_recv.at[1 + i, q], x_peer[k])

    def pass_on(q):
        for i, k in enumerate((1, 3)):
            s = slot(turn(x, 4 - k), core)
            arrive(rows_part(s, q), cross_recv.at[1 + i, q])
            piece = rows_ref.at[s, pl.ds(q * step + i * (step // 2), step // 2)]
            send(piece, piece, cross_send.at[2, q, i], cross_recv.at[3 + i, q], x_peer[k])

    def far_x(q):
        s = slot(turn(x, 2), core)
        for i in range(2):
            piece = rows_ref.at[s, pl.ds(q * step + i * (step // 2), step // 2)]
            arrive(piece, cross_recv.at[3 + i, q])

    def twin_rows(part, parts):
        size = half // parts
        for j in range(2):
            send(rows_ref.at[4 + j, pl.ds(part * size, size)],
                 rows_ref.at[2 * j + core, pl.ds(part * size, size)],
                 cross_send.at[3, part, j], cross_recv.at[5 + j, part], twin)

    def twin_rows_arrive(part, parts):
        size = half // parts
        for j in range(2):
            arrive(rows_ref.at[2 * j + 1 - core, pl.ds(part * size, size)],
                   cross_recv.at[5 + j, part])

    def pixel_rows(owner_row, start, count):
        return pixels_ref.at[pl.ds(owner_row * 64 + start, count)]

    def pixels_start():
        local = pltpu.make_async_copy(pixel_ref, pixel_rows(row, 0, 64), local_sem.at[0])
        local.start()
        for q in range(2):
            for i, k in enumerate((1, 3)):
                send(pixel_ref.at[pl.ds(32 * q, 32)], pixel_rows(row, 32 * q, 32),
                     pixel_send.at[0, q, i], pixel_recv.at[0, q, i], z_peer[k])
        send(pixel_ref, pixel_rows(row, 0, 64), pixel_send.at[2, 0, 0], pixel_recv.at[2, 0, 0], twin)
        return local

    def pixels_on(q):
        for i, k in enumerate((1, 3)):
            owner = turn(z, 4 - k) * 2 + core
            arrive(pixel_rows(owner, 32 * q, 32), pixel_recv.at[0, q, i])
            piece = pixel_rows(owner, 32 * q + 16 * i, 16)
            send(piece, piece, pixel_send.at[1, q, i], pixel_recv.at[1, q, i], z_peer[k])
            whole = pixel_rows(owner, 32 * q, 32)
            send(whole, whole, pixel_send.at[3, q, i], pixel_recv.at[3, q, i], twin)

    def pixels_far(q):
        owner = turn(z, 2) * 2 + core
        for i in range(2):
            piece = pixel_rows(owner, 32 * q + 16 * i, 16)
            arrive(piece, pixel_recv.at[1, q, i])
        whole = pixel_rows(owner, 32 * q, 32)
        send(whole, whole, pixel_send.at[4, q, 0], pixel_recv.at[4, q, 0], twin)

    def pixels_end():
        arrive(pixel_rows(z * 2 + 1 - core, 0, 64), pixel_recv.at[2, 0, 0])
        for q in range(2):
            for i, k in enumerate((1, 3)):
                arrive(pixel_rows(turn(z, 4 - k) * 2 + 1 - core, 32 * q, 32), pixel_recv.at[3, q, i])
            arrive(pixel_rows(turn(z, 2) * 2 + 1 - core, 32 * q, 32), pixel_recv.at[4, q, 0])

    def sector_columns(owner_row):
        return sector_ref.at[:, pl.ds(pl.multiple_of(owner_row * 128, 128), 128)]

    sector_peers = z_peer[1:] + other_z[1:] + [twin]
    peer_rows = [p[0] for p in sector_peers]

    def sectors_start():
        mine = sectors_ref.at[pl.ds(row * 64, 64)]
        local = pltpu.make_async_copy(sector_columns(row), mine, local_sem.at[1])
        local.start()
        for i, peer in enumerate(sector_peers):
            send(sector_columns(peer_rows[i]), mine, sector_send.at[i], sector_recv.at[i], peer)
        return local

    def sectors_end():
        for i in range(7):
            if i == 6:
                source = z * 2 + 1 - core
            else:
                other = (i // 3)
                back = turn(z, 4 - (i % 3 + 1))
                source = back * 2 + (core if other == 0 else 1 - core)
            arrive(sectors_ref.at[pl.ds(source * 64, 64)], sector_recv.at[i])

    for k in range(1, 16):
        source = row * 16 + turn(y, (16 - k) // 4 if k % 4 == 0 else 4 - k // 4) * 4 + turn(x, 4 - k % 4)
        arrive(all_ref.at[pl.ds(source, 1)], block_recv.at[k - 1])

    def block_part(zs, which):
        return all_ref.at[pl.ds(zs * 32 + which * 16, 16), :, pl.ds(0, 128 * (zs + 1))]

    def block_copies(zs):
        part = block_part(zs, core)
        return [
            pltpu.make_async_remote_copy(
                src_ref=part, dst_ref=part, send_sem=block_send.at[14 + k],
                recv_sem=block_recv.at[15 + zs], device_id=z_peer[k], device_id_type=MESH,
            )
            for k in (1, 2, 3)
        ]

    def block_twin(zs):
        part = block_part(zs, core)
        return pltpu.make_async_remote_copy(
            src_ref=part, dst_ref=part, send_sem=block_send.at[18 + zs],
            recv_sem=block_recv.at[19 + zs], device_id=twin, device_id_type=MESH,
        )

    for zs in range(4):
        @pl.when(z == zs)
        def _(zs=zs):
            for copy in block_copies(zs):
                copy.start()
            block_twin(zs).start()

    def block_relay(zs):
        @pl.when(z != zs)
        def _():
            arrive(block_part(zs, core), block_recv.at[15 + zs])
            block_twin(zs).start()

    def block_ready(zs):
        arrive(block_part(zs, 1 - core), block_recv.at[19 + zs])

    def load_rows(zs):
        width = 128 * (zs + 1)
        for i in range(32):
            m_ref[128 * zs + 4 * i : 128 * zs + 4 * i + 4, :width] = all_ref[32 * zs + i, :, :width]

    for q in range(CHUNKS):
        @pl.when(holds)
        def _(q=q):
            arrive(rows_part(my_slot, q), cross_recv.at[0, q])
            for i, k in enumerate((1, 3)):
                pltpu.make_async_remote_copy(
                    src_ref=rows_part(my_slot, q), dst_ref=rows_part(my_slot, q),
                    send_sem=cross_send.at[1, q, i], recv_sem=cross_recv.at[1 + i, q],
                    device_id=x_peer[k], device_id_type=MESH,
                ).start()

    def pass_x_other(q):
        @pl.when(jnp.logical_not(holds))
        def _():
            arrive(rows_part(my_slot, q), cross_recv.at[0, q])
            for i, k in enumerate((1, 3)):
                pltpu.make_async_remote_copy(
                    src_ref=rows_part(my_slot, q), dst_ref=rows_part(my_slot, q),
                    send_sem=cross_send.at[1, q, i], recv_sem=cross_recv.at[1 + i, q],
                    device_id=x_peer[k], device_id_type=MESH,
                ).start()

    block_relay(0)
    local = [pixels_start(), sectors_start()]
    block_ready(0)
    load_rows(0)

    def rest_of_block():
        for zs in (1, 2, 3):
            block_relay(zs)

    plan = {
        (0, 11): [rest_of_block, lambda: pass_x_other(0)],
        (0, 15): [lambda: [(block_ready(zs), load_rows(zs)) for zs in (1, 2, 3)]],
        (1, 3): [lambda: pass_x_other(1), lambda: pass_on(0), lambda: pixels_on(0)],
        (1, 11): [lambda: pass_x_other(2), lambda: pass_on(1)],
        (2, 3): [lambda: pass_x_other(3), lambda: pass_on(2), lambda: pixels_on(1), lambda: pixels_far(0)],
        (2, 11): [lambda: far_x(0), lambda: far_x(1), lambda: twin_rows(0, 2)],
        (3, 0): [lambda: pass_on(3)],
        (3, 7): [lambda: pixels_far(1)],
        (3, 15): [lambda: far_x(2), lambda: far_x(3), lambda: twin_rows(1, 2)],
    }

    n = inverse_ref.shape[0]
    inverse_ref[...] = jnp.zeros_like(inverse_ref)
    for b in range(n // 128):
        s, e = b * 128, b * 128 + 128

        def store(g, value):
            inverse_ref[s + 8 * g : s + 8 * g + 8, s:e] = value

        def after(g):
            for action in plan.get((b, g), ()):
                action()

        invert_tile(m_ref[s:e, s:e], store, after)
        inverse = inverse_ref[s:e, s:e]
        if b:
            inverse_ref[s:e, :s] = dot_nn(inverse, m_ref[s:e, :s])
        if e < n:
            below = dot_nt(m_ref[e:, s:e], inverse)
            m_ref[e:, e:] -= dot_nt(below, below)
            if b:
                m_ref[e:, :s] -= dot_nn(below, inverse_ref[s:e, :s])
            m_ref[e:, s:e] = -dot_nn(below, inverse)

    pixels_end()
    sectors_end()
    for part in range(2):
        twin_rows_arrive(part, 2)
    for copy in local:
        copy.wait()
    for copy in sent:
        copy.wait_send()

    @pl.when(holds)
    def _():
        for q in range(CHUNKS):
            for k in (1, 2, 3):
                y_copy(q, k).wait_send()

    for q in range(CHUNKS):
        for i, k in enumerate((1, 3)):
            part = rows_part(my_slot, q)
            pltpu.make_async_copy(part, part, cross_send.at[1, q, i]).wait()
    for zs in range(4):
        @pl.when(z == zs)
        def _(zs=zs):
            for copy in block_copies(zs):
                copy.wait_send()
        block_twin(zs).wait_send()


def panel(own, cross, pixels, sectors):
    dma = pltpu.SemaphoreType.DMA
    anywhere = pl.BlockSpec(memory_space=pltpu.HBM)
    return pl.pallas_call(
        panel_kernel,
        out_shape=(
            jax.ShapeDtypeStruct((512, 512), jnp.float32),
            jax.ShapeDtypeStruct((6, 256, 512), jnp.float32),
            jax.ShapeDtypeStruct((512, 2048), jnp.float32),
            jax.ShapeDtypeStruct((512, 128), jnp.float32),
        ),
        in_specs=[pl.BlockSpec(memory_space=pltpu.VMEM), anywhere, anywhere, anywhere],
        out_specs=(pl.BlockSpec(memory_space=pltpu.VMEM), anywhere, anywhere, anywhere),
        scratch_shapes=[
            pltpu.VMEM((128, 4, 512), jnp.float32),
            pltpu.VMEM((512, 512), jnp.float32),
            dma((22,)), dma((23,)),
            dma((4, CHUNKS, 3)), dma((7, CHUNKS)),
            dma((5, 2, 2)), dma((5, 2, 2)),
            dma((7,)), dma((7,)),
            dma((2,)),
        ],
        compiler_params=pltpu.CompilerParams(
            collective_id=0, has_side_effects=True, vmem_limit_bytes=32 << 20
        ),
        name="panel",
    )(own.reshape(1, 4, 512), cross, pixels, sectors)


def shards(
    panel_block, panel_cross, trail_block, panel_pixels, trail_pixels, panel_sectors, trail_sectors
):
    row_index = lax.axis_index("row")
    col_index = lax.axis_index("col")
    inverse, rows, pixels, sectors = panel(panel_block, panel_cross, panel_pixels, panel_sectors)
    cross_rows = rows[:4].reshape(1024, 512)

    def dot(a, b, ca, cb):
        return lax.dot_general(a, b, (((ca,), (cb,)), ((), ())), precision=lax.Precision.HIGH)

    n = inverse.shape[0]
    device_index = row_index * lax.axis_size("col") + col_index
    factor_rows = lax.dot_general(
        panel_block, inverse, (((1,), (1,)), ((), ())), precision=HIGHEST
    )
    own_row = device_index * 4 + lax.broadcasted_iota(jnp.int32, (4, n), 0)
    factor_rows = jnp.where(lax.broadcasted_iota(jnp.int32, (4, n), 1) <= own_row, factor_rows, 0.0)
    column_own = dot(panel_cross, inverse, 1, 1)
    row_block = dot(cross_rows, inverse, 1, 1)
    trail_updated = trail_block - dot(row_block, column_own, 1, 1)
    coupling = dot(row_block, inverse, 1, 0)
    pixel_total = trail_pixels - dot(coupling, pixels, 1, 0)
    solved = dot(inverse, sectors, 1, 0)
    kriging_weights = dot(inverse, solved, 0, 0)
    sectors_updated = trail_sectors - dot(column_own, solved, 1, 0)
    predicted = dot(pixels, kriging_weights, 0, 0)
    return (factor_rows, column_own, trail_updated, pixel_total, sectors_updated, predicted)


def solution(mesh):
    return jax.shard_map(
        shards,
        mesh=mesh,
        in_specs=(
            P(("row", "col"), None),
            P("col", None),
            P("row", "col"),
            P("row", "col"),
            P("row", "col"),
            P("row", None),
            P("col", "row"),
        ),
        out_specs=(
            P(("row", "col"), None),
            P("col", None),
            P("row", "col"),
            P("row", "col"),
            P("col", "row"),
            P("col", "row"),
        ),
        check_vma=False,
    )
```

```python
import functools

import jax
import jax.numpy as jnp
from jax import lax
from jax.experimental import pallas as pl
from jax.experimental.pallas import tpu as pltpu
from jax.sharding import PartitionSpec as P

HIGHEST = lax.Precision.HIGHEST
MESH = pl.DeviceIdType.MESH
TILE = (8, 128)
CHUNKS = 4


def dot_nn(a, b):
    return lax.dot_general(
        a, b, (((1,), (0,)), ((), ())), precision=HIGHEST, preferred_element_type=jnp.float32
    )


def dot_nt(a, b):
    return lax.dot_general(
        a, b, (((1,), (1,)), ((), ())), precision=HIGHEST, preferred_element_type=jnp.float32
    )


def invert_tile(block, store, after):
    lane = lax.broadcasted_iota(jnp.int32, TILE, 1)
    sub = lax.broadcasted_iota(jnp.int32, TILE, 0)
    here = [sub == j for j in range(8)]
    zero = jnp.zeros(TILE, jnp.float32)
    lane_all = lax.broadcasted_iota(jnp.int32, (128, 128), 1)

    for g in range(16):
        first = 8 * g
        top = block[:8]
        in_group = (lane >= first) & (lane < first + 8)
        unit = (lane - first == sub).astype(jnp.float32)
        pivot = [jnp.broadcast_to(top[:, first + k : first + k + 1], TILE) for k in range(8)]
        rest = lax.select(in_group, unit, top)
        inverse = zero
        for j in range(8):
            row = jnp.broadcast_to(rest[j : j + 1], TILE)
            entry = {k: jnp.broadcast_to(pivot[k][j : j + 1], TILE) for k in range(j, 8)}
            recip = 1.0 / entry[j]
            inverse = lax.select(here[j], row * lax.rsqrt(entry[j]), inverse)
            factor = lax.select(here[j], -recip, pivot[j] * recip)
            rest = lax.select(here[j], zero, rest) - factor * row
            for k in range(j + 1, 8):
                pivot[k] = lax.select(here[j], zero, pivot[k]) - factor * entry[k]
        store(g, lax.select(lane < first + 8, inverse, zero))
        if g < 15:
            below = block[8:]
            shape = below.shape
            lane_b = lane_all[: shape[0]]
            value = lax.select(
                (lane_b >= first) & (lane_b < first + 8), jnp.zeros(shape, jnp.float32), below
            )
            for k in range(8):
                value = value - jnp.broadcast_to(
                    below[:, first + k : first + k + 1], shape
                ) * jnp.broadcast_to(rest[k : k + 1], shape)
            block = value
        after(g)


def panel_kernel(
    own_ref, cross_ref, pixel_ref, sector_ref,
    inverse_ref, rows_ref, pixels_ref, sectors_ref,
    all_ref, m_ref, block_send, block_recv, cross_send, cross_recv, pixel_send, pixel_recv,
    sector_send, sector_recv, local_sem,
):
    row, col = lax.axis_index("row"), lax.axis_index("col")
    z, core = row // 2, lax.rem(row, 2)
    y, x = col // 4, lax.rem(col, 4)

    def turn(value, k):
        return lax.rem(value + k, 4)

    twin = (z * 2 + 1 - core, col)
    plane = [(row, turn(y, k // 4) * 4 + turn(x, k % 4)) for k in range(1, 16)]
    z_peer = [None] + [(turn(z, k) * 2 + core, col) for k in (1, 2, 3)]
    other_z = [None] + [(turn(z, k) * 2 + 1 - core, col) for k in (1, 2, 3)]
    x_peer = [None] + [(row, y * 4 + turn(x, k)) for k in (1, 2, 3)]
    y_peer = [None] + [(row, turn(y, k) * 4 + x) for k in (1, 2, 3)]

    barrier = pltpu.get_barrier_semaphore()
    partners = plane + z_peer[1:] + other_z[1:] + [twin]
    for peer in partners:
        pl.semaphore_signal(barrier, inc=1, device_id=peer, device_id_type=MESH)
    me = row * 16 + col
    all_ref[pl.ds(me, 1)] = own_ref[...]
    pl.semaphore_wait(barrier, len(partners))

    sent = []

    def send(src, dst, send_sem, recv_sem, peer, keep=True):
        copy = pltpu.make_async_remote_copy(
            src_ref=src, dst_ref=dst, send_sem=send_sem, recv_sem=recv_sem,
            device_id=peer, device_id_type=MESH,
        )
        copy.start()
        if keep:
            sent.append(copy)
        return copy

    def arrive(ref, sem):
        pltpu.make_async_copy(ref, ref, sem).wait()

    for k in range(1, 16):
        part = all_ref.at[pl.ds(me, 1)]
        send(part, part, block_send.at[k - 1], block_recv.at[k - 1], plane[k - 1])

    half = 256
    step = half // CHUNKS

    def slot(which, holder):
        same = 1 - jnp.abs(which // 2 - holder)
        odd = lax.rem(which, 2)
        return same * (2 * odd + holder) + (1 - same) * (4 + odd)

    holds = y == z
    my_slot = slot(x, core)

    def cross_part(q):
        return cross_ref.at[pl.ds(core * half + q * step, step)]

    def rows_part(s, q):
        return rows_ref.at[s, pl.ds(q * step, step)]

    def y_copy(q, k):
        return pltpu.make_async_remote_copy(
            src_ref=cross_part(q), dst_ref=rows_part(my_slot, q),
            send_sem=cross_send.at[0, q, k - 1], recv_sem=cross_recv.at[0, q],
            device_id=y_peer[k], device_id_type=MESH,
        )

    def own_copy(q):
        return pltpu.make_async_copy(cross_part(q), rows_part(my_slot, q), cross_recv.at[0, q])

    @pl.when(holds)
    def _():
        for q in range(CHUNKS):
            own_copy(q).start()
        for q in range(CHUNKS):
            for k in (1, 3, 2):
                y_copy(q, k).start()

    def pass_x(q):
        arrive(rows_part(my_slot, q), cross_recv.at[0, q])
        for i, k in enumerate((1, 3)):
            send(rows_part(my_slot, q), rows_part(my_slot, q),
                 cross_send.at[1, q, i], cross_recv.at[1 + i, q], x_peer[k])

    def pass_on(q):
        for i, k in enumerate((1, 3)):
            s = slot(turn(x, 4 - k), core)
            arrive(rows_part(s, q), cross_recv.at[1 + i, q])
            piece = rows_ref.at[s, pl.ds(q * step + i * (step // 2), step // 2)]
            send(piece, piece, cross_send.at[2, q, i], cross_recv.at[3 + i, q], x_peer[k])

    def far_x(q):
        s = slot(turn(x, 2), core)
        for i in range(2):
            piece = rows_ref.at[s, pl.ds(q * step + i * (step // 2), step // 2)]
            arrive(piece, cross_recv.at[3 + i, q])

    def twin_rows(part, parts):
        size = half // parts
        for j in range(2):
            send(rows_ref.at[4 + j, pl.ds(part * size, size)],
                 rows_ref.at[2 * j + core, pl.ds(part * size, size)],
                 cross_send.at[3, part, j], cross_recv.at[5 + j, part], twin)

    def twin_rows_arrive(part, parts):
        size = half // parts
        for j in range(2):
            arrive(rows_ref.at[2 * j + 1 - core, pl.ds(part * size, size)],
                   cross_recv.at[5 + j, part])

    def pixel_rows(owner_row, start, count):
        return pixels_ref.at[pl.ds(owner_row * 64 + start, count)]

    def pixels_start():
        local = pltpu.make_async_copy(pixel_ref, pixel_rows(row, 0, 64), local_sem.at[0])
        local.start()
        for q in range(2):
            for i, k in enumerate((1, 3)):
                send(pixel_ref.at[pl.ds(32 * q, 32)], pixel_rows(row, 32 * q, 32),
                     pixel_send.at[0, q, i], pixel_recv.at[0, q, i], z_peer[k])
        send(pixel_ref, pixel_rows(row, 0, 64), pixel_send.at[2, 0, 0], pixel_recv.at[2, 0, 0], twin)
        return local

    def pixels_on(q):
        for i, k in enumerate((1, 3)):
            owner = turn(z, 4 - k) * 2 + core
            arrive(pixel_rows(owner, 32 * q, 32), pixel_recv.at[0, q, i])
            piece = pixel_rows(owner, 32 * q + 16 * i, 16)
            send(piece, piece, pixel_send.at[1, q, i], pixel_recv.at[1, q, i], z_peer[k])
            whole = pixel_rows(owner, 32 * q, 32)
            send(whole, whole, pixel_send.at[3, q, i], pixel_recv.at[3, q, i], twin)

    def pixels_far(q):
        owner = turn(z, 2) * 2 + core
        for i in range(2):
            piece = pixel_rows(owner, 32 * q + 16 * i, 16)
            arrive(piece, pixel_recv.at[1, q, i])
        whole = pixel_rows(owner, 32 * q, 32)
        send(whole, whole, pixel_send.at[4, q, 0], pixel_recv.at[4, q, 0], twin)

    def pixels_end():
        arrive(pixel_rows(z * 2 + 1 - core, 0, 64), pixel_recv.at[2, 0, 0])
        for q in range(2):
            for i, k in enumerate((1, 3)):
                arrive(pixel_rows(turn(z, 4 - k) * 2 + 1 - core, 32 * q, 32), pixel_recv.at[3, q, i])
            arrive(pixel_rows(turn(z, 2) * 2 + 1 - core, 32 * q, 32), pixel_recv.at[4, q, 0])

    def sector_columns(owner_row):
        return sector_ref.at[:, pl.ds(pl.multiple_of(owner_row * 128, 128), 128)]

    sector_peers = z_peer[1:] + other_z[1:] + [twin]
    peer_rows = [p[0] for p in sector_peers]

    def sectors_start():
        mine = sectors_ref.at[pl.ds(row * 64, 64)]
        local = pltpu.make_async_copy(sector_columns(row), mine, local_sem.at[1])
        local.start()
        for i, peer in enumerate(sector_peers):
            send(sector_columns(peer_rows[i]), mine, sector_send.at[i], sector_recv.at[i], peer)
        return local

    def sectors_end():
        for i in range(7):
            if i == 6:
                source = z * 2 + 1 - core
            else:
                other = (i // 3)
                back = turn(z, 4 - (i % 3 + 1))
                source = back * 2 + (core if other == 0 else 1 - core)
            arrive(sectors_ref.at[pl.ds(source * 64, 64)], sector_recv.at[i])

    for k in range(1, 16):
        source = row * 16 + turn(y, (16 - k) // 4 if k % 4 == 0 else 4 - k // 4) * 4 + turn(x, 4 - k % 4)
        arrive(all_ref.at[pl.ds(source, 1)], block_recv.at[k - 1])

    def block_part(zs, which):
        return all_ref.at[pl.ds(zs * 32 + which * 16, 16), :, pl.ds(0, 128 * (zs + 1))]

    def block_copies(zs):
        part = block_part(zs, core)
        return [
            pltpu.make_async_remote_copy(
                src_ref=part, dst_ref=part, send_sem=block_send.at[14 + k],
                recv_sem=block_recv.at[15 + zs], device_id=z_peer[k], device_id_type=MESH,
            )
            for k in (1, 2, 3)
        ]

    def block_twin(zs):
        part = block_part(zs, core)
        return pltpu.make_async_remote_copy(
            src_ref=part, dst_ref=part, send_sem=block_send.at[18 + zs],
            recv_sem=block_recv.at[19 + zs], device_id=twin, device_id_type=MESH,
        )

    for zs in range(4):
        @pl.when(z == zs)
        def _(zs=zs):
            for copy in block_copies(zs):
                copy.start()
            block_twin(zs).start()

    local = [pixels_start()]

    def block_relay(zs):
        @pl.when(z != zs)
        def _():
            arrive(block_part(zs, core), block_recv.at[15 + zs])
            block_twin(zs).start()

    def block_ready(zs):
        arrive(block_part(zs, 1 - core), block_recv.at[19 + zs])

    def load_rows(zs):
        width = 128 * (zs + 1)
        for i in range(32):
            m_ref[128 * zs + 4 * i : 128 * zs + 4 * i + 4, :width] = all_ref[32 * zs + i, :, :width]

    for q in range(CHUNKS):
        @pl.when(holds)
        def _(q=q):
            arrive(rows_part(my_slot, q), cross_recv.at[0, q])
            for i, k in enumerate((1, 3)):
                pltpu.make_async_remote_copy(
                    src_ref=rows_part(my_slot, q), dst_ref=rows_part(my_slot, q),
                    send_sem=cross_send.at[1, q, i], recv_sem=cross_recv.at[1 + i, q],
                    device_id=x_peer[k], device_id_type=MESH,
                ).start()

    def pass_x_other(q):
        @pl.when(jnp.logical_not(holds))
        def _():
            arrive(rows_part(my_slot, q), cross_recv.at[0, q])
            for i, k in enumerate((1, 3)):
                pltpu.make_async_remote_copy(
                    src_ref=rows_part(my_slot, q), dst_ref=rows_part(my_slot, q),
                    send_sem=cross_send.at[1, q, i], recv_sem=cross_recv.at[1 + i, q],
                    device_id=x_peer[k], device_id_type=MESH,
                ).start()

    block_relay(0)
    block_ready(0)
    load_rows(0)
    local.append(sectors_start())
    pass_x_other(0)

    def rest_of_block():
        for zs in (1, 2, 3):
            block_relay(zs)

    plan = {
        (0, 7): [lambda: pass_x_other(1)],
        (0, 11): [rest_of_block],
        (0, 15): [lambda: [(block_ready(zs), load_rows(zs)) for zs in (1, 2, 3)]],
        (1, 0): [lambda: pass_on(0)],
        (1, 3): [lambda: pass_x_other(2)],
        (1, 8): [lambda: pass_on(1)],
        (1, 10): [lambda: pixels_on(0)],
        (1, 13): [lambda: pixels_on(1)],
        (1, 15): [lambda: pass_x_other(3)],
        (2, 4): [lambda: pass_on(2), lambda: far_x(0)],
        (2, 10): [lambda: far_x(1), lambda: twin_rows(0, 2)],
        (2, 15): [lambda: pass_on(3)],
        (3, 0): [lambda: pixels_far(0)],
        (3, 4): [lambda: pixels_far(1)],
        (3, 8): [lambda: far_x(2)],
        (3, 12): [lambda: far_x(3), lambda: twin_rows(1, 2)],
    }

    n = inverse_ref.shape[0]
    inverse_ref[...] = jnp.zeros_like(inverse_ref)
    for b in range(n // 128):
        s, e = b * 128, b * 128 + 128

        def store(g, value):
            inverse_ref[s + 8 * g : s + 8 * g + 8, s:e] = value

        def after(g):
            for action in plan.get((b, g), ()):
                action()

        invert_tile(m_ref[s:e, s:e], store, after)
        inverse = inverse_ref[s:e, s:e]
        if b:
            inverse_ref[s:e, :s] = dot_nn(inverse, m_ref[s:e, :s])
        if e < n:
            below = dot_nt(m_ref[e:, s:e], inverse)
            m_ref[e:, e:] -= dot_nt(below, below)
            if b:
                m_ref[e:, :s] -= dot_nn(below, inverse_ref[s:e, :s])
            m_ref[e:, s:e] = -dot_nn(below, inverse)

    pixels_end()
    sectors_end()
    for part in range(2):
        twin_rows_arrive(part, 2)
    for copy in local:
        copy.wait()
    for copy in sent:
        copy.wait_send()

    @pl.when(holds)
    def _():
        for q in range(CHUNKS):
            for k in (1, 2, 3):
                y_copy(q, k).wait_send()

    for q in range(CHUNKS):
        for i, k in enumerate((1, 3)):
            part = rows_part(my_slot, q)
            pltpu.make_async_copy(part, part, cross_send.at[1, q, i]).wait()
    for zs in range(4):
        @pl.when(z == zs)
        def _(zs=zs):
            for copy in block_copies(zs):
                copy.wait_send()
        block_twin(zs).wait_send()


def panel(own, cross, pixels, sectors):
    dma = pltpu.SemaphoreType.DMA
    anywhere = pl.BlockSpec(memory_space=pl.ANY)
    return pl.pallas_call(
        panel_kernel,
        out_shape=(
            jax.ShapeDtypeStruct((512, 512), jnp.float32),
            jax.ShapeDtypeStruct((6, 256, 512), jnp.float32),
            jax.ShapeDtypeStruct((512, 2048), jnp.float32),
            jax.ShapeDtypeStruct((512, 128), jnp.float32),
        ),
        in_specs=[pl.BlockSpec(memory_space=pltpu.VMEM), anywhere, anywhere, anywhere],
        out_specs=(pl.BlockSpec(memory_space=pltpu.VMEM), anywhere, anywhere, anywhere),
        scratch_shapes=[
            pltpu.VMEM((128, 4, 512), jnp.float32),
            pltpu.VMEM((512, 512), jnp.float32),
            dma((22,)), dma((23,)),
            dma((4, CHUNKS, 3)), dma((7, CHUNKS)),
            dma((5, 2, 2)), dma((5, 2, 2)),
            dma((7,)), dma((7,)),
            dma((2,)),
        ],
        compiler_params=pltpu.CompilerParams(
            collective_id=0, has_side_effects=True, vmem_limit_bytes=16 << 20
        ),
        cost_estimate=pl.CostEstimate(
            flops=40_000_000_000, bytes_accessed=16 << 20, transcendentals=0
        ),
        name="panel",
    )(own.reshape(1, 4, 512), cross, pixels, sectors)


def high_low(value):
    high = value.astype(jnp.bfloat16)
    return high, (value - high.astype(jnp.float32)).astype(jnp.bfloat16)


def left_cat(value, axis=1):
    high, low = high_low(value)
    return jnp.concatenate([high, high, low], axis=axis)


def right_cat(value, axis):
    high, low = high_low(value)
    return jnp.concatenate([high, low, high], axis=axis)


def mxu(a, b, ca, cb):
    return lax.dot_general(a, b, (((ca,), (cb,)), ((), ())), preferred_element_type=jnp.float32)


def product_kernel(
    own_ref, cross_ref, rows_ref, inverse_ref, sectors_ref, trail_sectors_ref,
    trail_ref, pixels_ref, trail_pixels_ref,
    factor_out, columns_out, trail_out, pixels_out, sectors_out, predicted_out,
    rows_cat, columns_cat, coupling_cat, weights_cat,
):
    step = pl.program_id(0)
    device = lax.axis_index("row") * 16 + lax.axis_index("col")

    @pl.when(step == 0)
    def _():
        inverse = inverse_ref[...]
        by_column = right_cat(inverse, 1)
        by_row = right_cat(inverse, 0)
        own = mxu(left_cat(own_ref[...]), by_column, 1, 1)
        lane = lax.broadcasted_iota(jnp.int32, own.shape, 1)
        line = lax.broadcasted_iota(jnp.int32, own.shape, 0) + device * 4
        factor_out[...] = jnp.where(lane <= line, own, 0.0)
        columns = mxu(left_cat(cross_ref[...]), by_column, 1, 1)
        columns_out[...] = columns
        columns_cat[...] = right_cat(columns, 1)
        for i in range(4):
            part = slice(256 * i, 256 * i + 256)
            panel_rows = left_cat(mxu(left_cat(rows_ref[i]), by_column, 1, 1))
            rows_cat[part] = panel_rows
            coupling_cat[part] = left_cat(mxu(panel_rows, by_row, 1, 0))
        solved = mxu(left_cat(inverse), right_cat(sectors_ref[...], 0), 1, 0)
        solved_cat = right_cat(solved, 0)
        sectors_out[...] = trail_sectors_ref[...] - mxu(left_cat(columns), solved_cat, 1, 0)
        weights = mxu(left_cat(inverse.T), solved_cat, 1, 0)
        weights_cat[...] = left_cat(weights.T)

    width = pixels_out.shape[1]
    part = pl.ds(pl.multiple_of(step * width, width), width)
    tile = right_cat(pixels_ref[:, part], 0)
    pixels_out[...] = trail_pixels_ref[:, part] - mxu(coupling_cat[...], tile, 1, 0)
    predicted_out[...] = mxu(weights_cat[...], tile, 1, 0).T
    size = trail_out.shape[0]
    lines = pl.ds(pl.multiple_of(step * size, size), size)
    trail_out[...] = trail_ref[lines, :] - mxu(rows_cat[lines, :], columns_cat[...], 1, 1)


def products(own, cross, rows, inverse, sectors, trail_sectors, trail, pixels, trail_pixels):
    n, width = pixels.shape
    steps = 4
    height = trail.shape[0]

    def fixed(shape):
        return pl.BlockSpec(shape, lambda i: (0,) * len(shape), pipeline_mode=pl.Buffered(1))

    f32 = lambda *shape: jax.ShapeDtypeStruct(shape, jnp.float32)
    bf16 = lambda *shape: pltpu.VMEM(shape, jnp.bfloat16)
    return pl.pallas_call(
        product_kernel,
        grid=(steps,),
        out_shape=(
            f32(*own.shape), f32(*cross.shape), f32(*trail.shape), f32(*trail_pixels.shape),
            f32(*trail_sectors.shape), f32(width, sectors.shape[1]),
        ),
        in_specs=[pl.BlockSpec(memory_space=pltpu.VMEM)] * 9,
        out_specs=(
            fixed(own.shape), fixed(cross.shape),
            pl.BlockSpec((height // steps, trail.shape[1]), lambda i: (i, 0)),
            pl.BlockSpec((height, width // steps), lambda i: (0, i)),
            fixed(trail_sectors.shape),
            pl.BlockSpec((width // steps, sectors.shape[1]), lambda i: (i, 0)),
        ),
        scratch_shapes=[
            bf16(height, 3 * n), bf16(cross.shape[0], 3 * n), bf16(height, 3 * n),
            bf16(sectors.shape[1], 3 * n),
        ],
        compiler_params=pltpu.CompilerParams(vmem_limit_bytes=26 << 20),
        cost_estimate=pl.CostEstimate(
            flops=13_500_000_000, bytes_accessed=32 << 20, transcendentals=0
        ),
        name="products",
    )(own, cross, rows, inverse, sectors, trail_sectors, trail, pixels, trail_pixels)


def shards(
    panel_block, panel_cross, trail_block, panel_pixels, trail_pixels, panel_sectors, trail_sectors
):
    in_hbm = lambda v: pltpu.with_memory_space_constraint(v, pltpu.HBM)
    inverse, rows, pixels, sectors = panel(
        panel_block, in_hbm(panel_cross), in_hbm(panel_pixels), in_hbm(panel_sectors)
    )
    return products(
        panel_block, panel_cross, rows, inverse, sectors, trail_sectors, trail_block, pixels, trail_pixels
    )


def solution(mesh):
    return jax.shard_map(
        shards,
        mesh=mesh,
        in_specs=(
            P(("row", "col"), None),
            P("col", None),
            P("row", "col"),
            P("row", "col"),
            P("row", "col"),
            P("row", None),
            P("col", "row"),
        ),
        out_specs=(
            P(("row", "col"), None),
            P("col", None),
            P("row", "col"),
            P("row", "col"),
            P("col", "row"),
            P("col", "row"),
        ),
        check_vma=False,
    )
```

```python
import functools

import jax
import jax.numpy as jnp
from jax import lax
from jax.experimental import pallas as pl
from jax.experimental.pallas import tpu as pltpu
from jax.sharding import PartitionSpec as P

HIGHEST = lax.Precision.HIGHEST
MESH = pl.DeviceIdType.MESH
TILE = (8, 128)
CHUNKS = 4


def dot_nn(a, b):
    return lax.dot_general(
        a, b, (((1,), (0,)), ((), ())), precision=HIGHEST, preferred_element_type=jnp.float32
    )


def dot_nt(a, b):
    return lax.dot_general(
        a, b, (((1,), (1,)), ((), ())), precision=HIGHEST, preferred_element_type=jnp.float32
    )


def invert_tile(block, store, after):
    lane = lax.broadcasted_iota(jnp.int32, TILE, 1)
    sub = lax.broadcasted_iota(jnp.int32, TILE, 0)
    here = [sub == j for j in range(8)]
    zero = jnp.zeros(TILE, jnp.float32)
    lane_all = lax.broadcasted_iota(jnp.int32, (128, 128), 1)

    for g in range(16):
        first = 8 * g
        top = block[:8]
        in_group = (lane >= first) & (lane < first + 8)
        unit = (lane - first == sub).astype(jnp.float32)
        pivot = [jnp.broadcast_to(top[:, first + k : first + k + 1], TILE) for k in range(8)]
        entry = {
            (j, k): jnp.broadcast_to(pivot[k][j : j + 1], TILE) for k in range(8) for j in range(k + 1)
        }
        rest = lax.select(in_group, unit, top)
        inverse = zero
        for j in range(8):
            recip = 1.0 / entry[j, j]
            scaled = {k: entry[j, k] * recip for k in range(j + 1, 8)}
            for i in range(j + 1, 8):
                for k in range(i, 8):
                    entry[i, k] = entry[i, k] - scaled[i] * entry[j, k]
            row = jnp.broadcast_to(rest[j : j + 1], TILE)
            inverse = lax.select(here[j], row * lax.rsqrt(entry[j, j]), inverse)
            factor = lax.select(here[j], -recip, pivot[j] * recip)
            rest = lax.select(here[j], zero, rest) - factor * row
            for k in range(j + 1, 8):
                pivot[k] = lax.select(here[j], zero, pivot[k]) - factor * entry[j, k]
        store(g, lax.select(lane < first + 8, inverse, zero))
        if g < 15:
            below = block[8:]
            shape = below.shape
            lane_b = lane_all[: shape[0]]
            value = lax.select(
                (lane_b >= first) & (lane_b < first + 8), jnp.zeros(shape, jnp.float32), below
            )
            for k in range(8):
                value = value - jnp.broadcast_to(
                    below[:, first + k : first + k + 1], shape
                ) * jnp.broadcast_to(rest[k : k + 1], shape)
            block = value
        after(g)


def panel_kernel(
    own_ref, cross_ref, pixel_ref, sector_ref,
    inverse_ref, rows_ref, pixels_ref, sectors_ref,
    all_ref, m_ref, below_ref, block_send, block_recv, cross_send, cross_recv, pixel_send, pixel_recv,
    sector_send, sector_recv, local_sem,
):
    row, col = lax.axis_index("row"), lax.axis_index("col")
    z, core = row // 2, lax.rem(row, 2)
    y, x = col // 4, lax.rem(col, 4)

    def turn(value, k):
        return lax.rem(value + k, 4)

    twin = (z * 2 + 1 - core, col)
    plane = [(row, turn(y, k // 4) * 4 + turn(x, k % 4)) for k in range(1, 16)]
    z_peer = [None] + [(turn(z, k) * 2 + core, col) for k in (1, 2, 3)]
    other_z = [None] + [(turn(z, k) * 2 + 1 - core, col) for k in (1, 2, 3)]
    x_peer = [None] + [(row, y * 4 + turn(x, k)) for k in (1, 2, 3)]
    y_peer = [None] + [(row, turn(y, k) * 4 + x) for k in (1, 2, 3)]

    barrier = pltpu.get_barrier_semaphore()
    partners = plane + z_peer[1:] + other_z[1:] + [twin]
    for peer in partners:
        pl.semaphore_signal(barrier, inc=1, device_id=peer, device_id_type=MESH)
    me = row * 16 + col
    own_rows = pltpu.make_async_copy(own_ref, all_ref.at[pl.ds(me, 1)], local_sem.at[2])
    own_rows.start()
    pl.semaphore_wait(barrier, len(partners))

    sent = []

    def send(src, dst, send_sem, recv_sem, peer, keep=True):
        copy = pltpu.make_async_remote_copy(
            src_ref=src, dst_ref=dst, send_sem=send_sem, recv_sem=recv_sem,
            device_id=peer, device_id_type=MESH,
        )
        copy.start()
        if keep:
            sent.append(copy)
        return copy

    def arrive(ref, sem):
        pltpu.make_async_copy(ref, ref, sem).wait()

    for k in range(1, 16):
        part = all_ref.at[pl.ds(me, 1)]
        send(own_ref, part, block_send.at[k - 1], block_recv.at[k - 1], plane[k - 1])

    half = 256
    step = half // CHUNKS

    def slot(which, holder):
        same = 1 - jnp.abs(which // 2 - holder)
        odd = lax.rem(which, 2)
        return same * (2 * odd + holder) + (1 - same) * (4 + odd)

    holds = y == z
    my_slot = slot(x, core)

    def cross_part(q):
        return cross_ref.at[pl.ds(core * half + q * step, step)]

    def rows_part(s, q):
        return rows_ref.at[s, pl.ds(q * step, step)]

    def y_copy(q, k):
        return pltpu.make_async_remote_copy(
            src_ref=cross_part(q), dst_ref=rows_part(my_slot, q),
            send_sem=cross_send.at[0, q, k - 1], recv_sem=cross_recv.at[0, q],
            device_id=y_peer[k], device_id_type=MESH,
        )

    def own_copy(q):
        return pltpu.make_async_copy(cross_part(q), rows_part(my_slot, q), cross_recv.at[0, q])

    @pl.when(holds)
    def _():
        for q in range(CHUNKS):
            own_copy(q).start()
        for q in range(CHUNKS):
            for k in (1, 3, 2):
                y_copy(q, k).start()

    def pass_x(q):
        arrive(rows_part(my_slot, q), cross_recv.at[0, q])
        for i, k in enumerate((1, 3)):
            send(rows_part(my_slot, q), rows_part(my_slot, q),
                 cross_send.at[1, q, i], cross_recv.at[1 + i, q], x_peer[k])

    def pass_on(q):
        for i, k in enumerate((1, 3)):
            s = slot(turn(x, 4 - k), core)
            arrive(rows_part(s, q), cross_recv.at[1 + i, q])
            piece = rows_ref.at[s, pl.ds(q * step + i * (step // 2), step // 2)]
            send(piece, piece, cross_send.at[2, q, i], cross_recv.at[3 + i, q], x_peer[k])

    def far_x(q):
        s = slot(turn(x, 2), core)
        for i in range(2):
            piece = rows_ref.at[s, pl.ds(q * step + i * (step // 2), step // 2)]
            arrive(piece, cross_recv.at[3 + i, q])

    def twin_rows(part, parts):
        size = half // parts
        for j in range(2):
            send(rows_ref.at[4 + j, pl.ds(part * size, size)],
                 rows_ref.at[2 * j + core, pl.ds(part * size, size)],
                 cross_send.at[3, part, j], cross_recv.at[5 + j, part], twin)

    def twin_rows_arrive(part, parts):
        size = half // parts
        for j in range(2):
            arrive(rows_ref.at[2 * j + 1 - core, pl.ds(part * size, size)],
                   cross_recv.at[5 + j, part])

    def pixel_rows(owner_row, start, count):
        return pixels_ref.at[pl.ds(owner_row * 64 + start, count)]

    def pixels_start():
        local = pltpu.make_async_copy(pixel_ref, pixel_rows(row, 0, 64), local_sem.at[0])
        local.start()
        for q in range(1):
            for i, k in enumerate((1, 3)):
                send(pixel_ref, pixel_rows(row, 0, 64),
                     pixel_send.at[0, q, i], pixel_recv.at[0, q, i], z_peer[k])
        send(pixel_ref, pixel_rows(row, 0, 64), pixel_send.at[2, 0, 0], pixel_recv.at[2, 0, 0], twin)
        return local

    def pixels_on(q):
        for i, k in enumerate((1, 3)):
            owner = turn(z, 4 - k) * 2 + core
            arrive(pixel_rows(owner, 0, 64), pixel_recv.at[0, q, i])
            piece = pixel_rows(owner, 32 * i, 32)
            send(piece, piece, pixel_send.at[1, q, i], pixel_recv.at[1, q, i], z_peer[k])
            whole = pixel_rows(owner, 0, 64)
            send(whole, whole, pixel_send.at[3, q, i], pixel_recv.at[3, q, i], twin)

    def pixels_far(q):
        owner = turn(z, 2) * 2 + core
        for i in range(2):
            piece = pixel_rows(owner, 32 * i, 32)
            arrive(piece, pixel_recv.at[1, q, i])
        whole = pixel_rows(owner, 0, 64)
        send(whole, whole, pixel_send.at[4, q, 0], pixel_recv.at[4, q, 0], twin)

    def pixels_end():
        arrive(pixel_rows(z * 2 + 1 - core, 0, 64), pixel_recv.at[2, 0, 0])
        for q in range(1):
            for i, k in enumerate((1, 3)):
                arrive(pixel_rows(turn(z, 4 - k) * 2 + 1 - core, 0, 64), pixel_recv.at[3, q, i])
            arrive(pixel_rows(turn(z, 2) * 2 + 1 - core, 0, 64), pixel_recv.at[4, q, 0])

    def sector_columns(owner_row):
        return sector_ref.at[:, pl.ds(pl.multiple_of(owner_row * 128, 128), 128)]

    sector_peers = z_peer[1:] + other_z[1:] + [twin]
    peer_rows = [p[0] for p in sector_peers]

    def sectors_start():
        mine = sectors_ref.at[pl.ds(row * 64, 64)]
        local = pltpu.make_async_copy(sector_columns(row), mine, local_sem.at[1])
        local.start()
        for i, peer in enumerate(sector_peers):
            send(sector_columns(peer_rows[i]), mine, sector_send.at[i], sector_recv.at[i], peer)
        return local

    def sectors_end():
        for i in range(7):
            if i == 6:
                source = z * 2 + 1 - core
            else:
                other = (i // 3)
                back = turn(z, 4 - (i % 3 + 1))
                source = back * 2 + (core if other == 0 else 1 - core)
            arrive(sectors_ref.at[pl.ds(source * 64, 64)], sector_recv.at[i])

    for k in range(1, 16):
        source = row * 16 + turn(y, (16 - k) // 4 if k % 4 == 0 else 4 - k // 4) * 4 + turn(x, 4 - k % 4)
        arrive(all_ref.at[pl.ds(source, 1)], block_recv.at[k - 1])

    own_rows.wait()

    def block_part(zs, which):
        return all_ref.at[pl.ds(zs * 32 + which * 16, 16), :, pl.ds(0, 128 * (zs + 1))]

    def block_copies(zs):
        part = block_part(zs, core)
        return [
            pltpu.make_async_remote_copy(
                src_ref=part, dst_ref=part, send_sem=block_send.at[14 + k],
                recv_sem=block_recv.at[15 + zs], device_id=z_peer[k], device_id_type=MESH,
            )
            for k in (1, 2, 3)
        ]

    def block_twin(zs):
        part = block_part(zs, core)
        return pltpu.make_async_remote_copy(
            src_ref=part, dst_ref=part, send_sem=block_send.at[18 + zs],
            recv_sem=block_recv.at[19 + zs], device_id=twin, device_id_type=MESH,
        )

    for zs in range(4):
        @pl.when(z == zs)
        def _(zs=zs):
            for copy in block_copies(zs):
                copy.start()
            block_twin(zs).start()

    local = [pixels_start()]

    def block_relay(zs):
        @pl.when(z != zs)
        def _():
            arrive(block_part(zs, core), block_recv.at[15 + zs])
            block_twin(zs).start()

    def block_ready(zs):
        arrive(block_part(zs, 1 - core), block_recv.at[19 + zs])

    def load_rows(zs):
        width = 128 * (zs + 1)
        for i in range(32):
            m_ref[128 * zs + 4 * i : 128 * zs + 4 * i + 4, :width] = all_ref[32 * zs + i, :, :width]

    for q in range(CHUNKS):
        @pl.when(holds)
        def _(q=q):
            arrive(rows_part(my_slot, q), cross_recv.at[0, q])
            for i, k in enumerate((1, 3)):
                pltpu.make_async_remote_copy(
                    src_ref=rows_part(my_slot, q), dst_ref=rows_part(my_slot, q),
                    send_sem=cross_send.at[1, q, i], recv_sem=cross_recv.at[1 + i, q],
                    device_id=x_peer[k], device_id_type=MESH,
                ).start()

    def pass_x_other(q):
        @pl.when(jnp.logical_not(holds))
        def _():
            arrive(rows_part(my_slot, q), cross_recv.at[0, q])
            for i, k in enumerate((1, 3)):
                pltpu.make_async_remote_copy(
                    src_ref=rows_part(my_slot, q), dst_ref=rows_part(my_slot, q),
                    send_sem=cross_send.at[1, q, i], recv_sem=cross_recv.at[1 + i, q],
                    device_id=x_peer[k], device_id_type=MESH,
                ).start()

    local.append(sectors_start())
    block_relay(0)
    pass_x_other(0)
    block_ready(0)
    load_rows(0)

    def rest_of_block():
        for zs in (1, 2, 3):
            block_relay(zs)

    plan = {
        (0, 7): [lambda: pass_x_other(1)],
        (0, 11): [rest_of_block],
        (0, 15): [lambda: [(block_ready(zs), load_rows(zs)) for zs in (1, 2, 3)]],
        (1, 0): [lambda: pass_on(0)],
        (1, 3): [lambda: pass_x_other(2)],
        (1, 8): [lambda: pass_on(1)],
        (1, 14): [lambda: pixels_on(0)],
        (1, 15): [lambda: pass_x_other(3)],
        (2, 4): [lambda: pass_on(2), lambda: far_x(0)],
        (2, 10): [lambda: far_x(1), lambda: twin_rows(0, 2)],
        (2, 15): [lambda: pass_on(3)],
        (3, 4): [lambda: pixels_far(0)],
        (3, 8): [lambda: far_x(2)],
        (3, 12): [lambda: far_x(3), lambda: twin_rows(1, 2)],
    }

    n = inverse_ref.shape[0]
    inverse_ref[...] = jnp.zeros_like(inverse_ref)
    later = []
    for b in range(n // 128):
        s, e = b * 128, b * 128 + 128
        jobs, later = later, []

        def store(g, value):
            inverse_ref[s + 8 * g : s + 8 * g + 8, s:e] = value

        def after(g):
            if g == 0:
                for job in jobs:
                    job()
            for action in plan.get((b, g), ()):
                action()

        invert_tile(m_ref[s:e, s:e], store, after)

        if e < n:
            below_ref[e:] = dot_nt(m_ref[e:, s:e], inverse_ref[s:e, s:e])
            near = below_ref[e : e + 128]
            m_ref[e : e + 128, e : e + 128] -= dot_nt(near, near)

        def finish_row(s=s, e=e):
            inverse_ref[s:e, :s] = dot_nn(inverse_ref[s:e, s:e], m_ref[s:e, :s])

        def update_rest(s=s, e=e):
            m_ref[e + 128 :, e:] -= dot_nt(below_ref[e + 128 :], below_ref[e:])

        def update_left(s=s, e=e):
            m_ref[e:, :s] -= dot_nn(below_ref[e:], inverse_ref[s:e, :s])

        def update_here(s=s, e=e):
            m_ref[e:, s:e] = -dot_nn(below_ref[e:], inverse_ref[s:e, s:e])

        if b:
            later.append(finish_row)
        if e < n:
            if e + 128 < n:
                later.append(update_rest)
            if b:
                later.append(update_left)
            later.append(update_here)
    for job in later:
        job()

    pixels_end()
    sectors_end()
    for part in range(2):
        twin_rows_arrive(part, 2)
    for copy in local:
        copy.wait()
    for copy in sent:
        copy.wait_send()

    @pl.when(holds)
    def _():
        for q in range(CHUNKS):
            for k in (1, 2, 3):
                y_copy(q, k).wait_send()

    for q in range(CHUNKS):
        for i, k in enumerate((1, 3)):
            part = rows_part(my_slot, q)
            pltpu.make_async_copy(part, part, cross_send.at[1, q, i]).wait()
    for zs in range(4):
        @pl.when(z == zs)
        def _(zs=zs):
            for copy in block_copies(zs):
                copy.wait_send()
        block_twin(zs).wait_send()


def panel(own, cross, pixels, sectors):
    dma = pltpu.SemaphoreType.DMA
    anywhere = pl.BlockSpec(memory_space=pl.ANY)
    return pl.pallas_call(
        panel_kernel,
        out_shape=(
            jax.ShapeDtypeStruct((512, 512), jnp.float32),
            jax.ShapeDtypeStruct((6, 256, 512), jnp.float32),
            jax.ShapeDtypeStruct((512, 2048), jnp.float32),
            jax.ShapeDtypeStruct((512, 128), jnp.float32),
        ),
        in_specs=[anywhere] * 4,
        out_specs=(pl.BlockSpec(memory_space=pltpu.VMEM), anywhere, anywhere, anywhere),
        scratch_shapes=[
            pltpu.VMEM((128, 4, 512), jnp.float32),
            pltpu.VMEM((512, 512), jnp.float32),
            pltpu.VMEM((512, 128), jnp.float32),
            dma((22,)), dma((23,)),
            dma((4, CHUNKS, 3)), dma((7, CHUNKS)),
            dma((5, 2, 2)), dma((5, 2, 2)),
            dma((7,)), dma((7,)),
            dma((3,)),
        ],
        compiler_params=pltpu.CompilerParams(
            collective_id=0, has_side_effects=True, vmem_limit_bytes=16 << 20
        ),
        cost_estimate=pl.CostEstimate(
            flops=40_000_000_000, bytes_accessed=16 << 20, transcendentals=0
        ),
        name="panel",
    )(own, cross, pixels, sectors)


def high_low(value):
    high = value.astype(jnp.bfloat16)
    return high, (value - high.astype(jnp.float32)).astype(jnp.bfloat16)


def left_cat(value, axis=1):
    high, low = high_low(value)
    return jnp.concatenate([high, high, low], axis=axis)


def right_cat(value, axis):
    high, low = high_low(value)
    return jnp.concatenate([high, low, high], axis=axis)


def mxu(a, b, ca, cb):
    return lax.dot_general(a, b, (((ca,), (cb,)), ((), ())), preferred_element_type=jnp.float32)


def product_kernel(
    own_ref, cross_ref, rows_ref, inverse_ref, sectors_ref, trail_sectors_ref,
    trail_ref, pixels_ref, trail_pixels_ref,
    factor_out, columns_out, trail_out, pixels_out, sectors_out, predicted_out,
    rows_cat, columns_cat, coupling_cat, weights_cat,
):
    step = pl.program_id(0)
    device = lax.axis_index("row") * 16 + lax.axis_index("col")

    @pl.when(step == 0)
    def _():
        inverse = inverse_ref[...]
        by_column = right_cat(inverse, 1)
        by_row = right_cat(inverse, 0)
        own = mxu(left_cat(own_ref[...]), by_column, 1, 1)
        lane = lax.broadcasted_iota(jnp.int32, own.shape, 1)
        line = lax.broadcasted_iota(jnp.int32, own.shape, 0) + device * 4
        factor_out[...] = jnp.where(lane <= line, own, 0.0)
        lower = right_cat(inverse[:256, :256], 1)
        last = right_cat(inverse[256:, 256:], 0)

        def times_upper(value):
            high, low = high_low(value)
            near = jnp.concatenate([high[:, :256], high[:, :256], low[:, :256]], axis=1)
            full = jnp.concatenate([high, high, low], axis=1)
            return jnp.concatenate(
                [mxu(near, lower, 1, 1), mxu(full, by_column[256:], 1, 1)], axis=1
            )

        columns = times_upper(cross_ref[...])
        columns_out[...] = columns
        columns_cat[...] = right_cat(columns, 1)
        for i in range(4):
            part = slice(256 * i, 256 * i + 256)
            high, low = high_low(times_upper(rows_ref[i]))
            panel_rows = jnp.concatenate([high, high, low], axis=1)
            rows_cat[part] = panel_rows
            far = jnp.concatenate([high[:, 256:], high[:, 256:], low[:, 256:]], axis=1)
            coupling_cat[part] = left_cat(jnp.concatenate(
                [mxu(panel_rows, by_row[:, :256], 1, 0), mxu(far, last, 1, 0)], axis=1
            ))
        solved = mxu(left_cat(inverse), right_cat(sectors_ref[...], 0), 1, 0)
        solved_cat = right_cat(solved, 0)
        sectors_out[...] = trail_sectors_ref[...] - mxu(left_cat(columns), solved_cat, 1, 0)
        weights = mxu(left_cat(inverse.T), solved_cat, 1, 0)
        weights_cat[...] = left_cat(weights.T)

    width = pixels_out.shape[1]
    part = pl.ds(pl.multiple_of(step * width, width), width)
    tile = right_cat(pixels_ref[:, part], 0)
    pixels_out[...] = trail_pixels_ref[:, part] - mxu(coupling_cat[...], tile, 1, 0)
    predicted_out[...] = mxu(weights_cat[...], tile, 1, 0).T
    size = trail_out.shape[0]
    lines = pl.ds(pl.multiple_of(step * size, size), size)
    trail_out[...] = trail_ref[lines, :] - mxu(rows_cat[lines, :], columns_cat[...], 1, 1)


def products(own, cross, rows, inverse, sectors, trail_sectors, trail, pixels, trail_pixels):
    n, width = pixels.shape
    steps = 4
    height = trail.shape[0]

    def fixed(shape):
        return pl.BlockSpec(shape, lambda i: (0,) * len(shape), pipeline_mode=pl.Buffered(1))

    f32 = lambda *shape: jax.ShapeDtypeStruct(shape, jnp.float32)
    bf16 = lambda *shape: pltpu.VMEM(shape, jnp.bfloat16)
    return pl.pallas_call(
        product_kernel,
        grid=(steps,),
        out_shape=(
            f32(*own.shape), f32(*cross.shape), f32(*trail.shape), f32(*trail_pixels.shape),
            f32(*trail_sectors.shape), f32(width, sectors.shape[1]),
        ),
        in_specs=[pl.BlockSpec(memory_space=pltpu.VMEM)] * 9,
        out_specs=(
            fixed(own.shape), fixed(cross.shape),
            pl.BlockSpec((height // steps, trail.shape[1]), lambda i: (i, 0)),
            pl.BlockSpec((height, width // steps), lambda i: (0, i)),
            fixed(trail_sectors.shape),
            pl.BlockSpec((width // steps, sectors.shape[1]), lambda i: (i, 0)),
        ),
        scratch_shapes=[
            bf16(height, 3 * n), bf16(cross.shape[0], 3 * n), bf16(height, 3 * n),
            bf16(sectors.shape[1], 3 * n),
        ],
        compiler_params=pltpu.CompilerParams(vmem_limit_bytes=26 << 20),
        cost_estimate=pl.CostEstimate(
            flops=13_500_000_000, bytes_accessed=32 << 20, transcendentals=0
        ),
        name="products",
    )(own, cross, rows, inverse, sectors, trail_sectors, trail, pixels, trail_pixels)


def shards(
    panel_block, panel_cross, trail_block, panel_pixels, trail_pixels, panel_sectors, trail_sectors
):
    in_hbm = lambda v: pltpu.with_memory_space_constraint(v, pltpu.HBM)
    inverse, rows, pixels, sectors = panel(
        in_hbm(panel_block.reshape(1, 4, 512)), in_hbm(panel_cross), in_hbm(panel_pixels), in_hbm(panel_sectors)
    )
    return products(
        panel_block, panel_cross, rows, inverse, sectors, trail_sectors, trail_block, pixels, trail_pixels
    )


def solution(mesh):
    return jax.shard_map(
        shards,
        mesh=mesh,
        in_specs=(
            P(("row", "col"), None),
            P("col", None),
            P("row", "col"),
            P("row", "col"),
            P("row", "col"),
            P("row", None),
            P("col", "row"),
        ),
        out_specs=(
            P(("row", "col"), None),
            P("col", None),
            P("row", "col"),
            P("row", "col"),
            P("col", "row"),
            P("col", "row"),
        ),
        check_vma=False,
    )
```

```python
import functools

import jax
import jax.numpy as jnp
from jax import lax
from jax.experimental import pallas as pl
from jax.experimental.pallas import tpu as pltpu
from jax.sharding import PartitionSpec as P

HIGHEST = lax.Precision.HIGHEST
MESH = pl.DeviceIdType.MESH
TILE = (8, 128)
CHUNKS = 4


def dot_nn(a, b):
    return lax.dot_general(
        a, b, (((1,), (0,)), ((), ())), precision=HIGHEST, preferred_element_type=jnp.float32
    )


def dot_nt(a, b):
    return lax.dot_general(
        a, b, (((1,), (1,)), ((), ())), precision=HIGHEST, preferred_element_type=jnp.float32
    )


def invert_tile(block, store, after):
    lane = lax.broadcasted_iota(jnp.int32, TILE, 1)
    sub = lax.broadcasted_iota(jnp.int32, TILE, 0)
    here = [sub == j for j in range(8)]
    zero = jnp.zeros(TILE, jnp.float32)
    lane_all = lax.broadcasted_iota(jnp.int32, (128, 128), 1)

    for g in range(16):
        first = 8 * g
        top = block[:8]
        in_group = (lane >= first) & (lane < first + 8)
        unit = (lane - first == sub).astype(jnp.float32)
        pivot = [jnp.broadcast_to(top[:, first + k : first + k + 1], TILE) for k in range(8)]
        entry = {
            (j, k): jnp.broadcast_to(pivot[k][j : j + 1], TILE) for k in range(8) for j in range(k + 1)
        }
        rest = lax.select(in_group, unit, top)
        inverse = zero
        for j in range(8):
            recip = 1.0 / entry[j, j]
            scaled = {k: entry[j, k] * recip for k in range(j + 1, 8)}
            for i in range(j + 1, 8):
                for k in range(i, 8):
                    entry[i, k] = entry[i, k] - scaled[i] * entry[j, k]
            row = jnp.broadcast_to(rest[j : j + 1], TILE)
            inverse = lax.select(here[j], row * lax.rsqrt(entry[j, j]), inverse)
            factor = lax.select(here[j], -recip, pivot[j] * recip)
            rest = lax.select(here[j], zero, rest) - factor * row
            for k in range(j + 1, 8):
                pivot[k] = lax.select(here[j], zero, pivot[k]) - factor * entry[j, k]
        store(g, lax.select(lane < first + 8, inverse, zero))
        if g < 15:
            below = block[8:]
            shape = below.shape
            lane_b = lane_all[: shape[0]]
            value = lax.select(
                (lane_b >= first) & (lane_b < first + 8), jnp.zeros(shape, jnp.float32), below
            )
            for k in range(8):
                value = value - jnp.broadcast_to(
                    below[:, first + k : first + k + 1], shape
                ) * jnp.broadcast_to(rest[k : k + 1], shape)
            block = value
        after(g)


def panel_kernel(
    own_ref, cross_ref, pixel_ref, sector_ref,
    inverse_ref, rows_ref, pixels_ref, sectors_ref,
    all_ref, m_ref, below_ref, block_send, block_recv, cross_send, cross_recv, pixel_send, pixel_recv,
    sector_send, sector_recv, local_sem,
):
    row, col = lax.axis_index("row"), lax.axis_index("col")
    z, core = row // 2, lax.rem(row, 2)
    y, x = col // 4, lax.rem(col, 4)

    def turn(value, k):
        return lax.rem(value + k, 4)

    twin = (z * 2 + 1 - core, col)
    plane = [(row, turn(y, k // 4) * 4 + turn(x, k % 4)) for k in range(1, 16)]
    z_peer = [None] + [(turn(z, k) * 2 + core, col) for k in (1, 2, 3)]
    other_z = [None] + [(turn(z, k) * 2 + 1 - core, col) for k in (1, 2, 3)]
    x_peer = [None] + [(row, y * 4 + turn(x, k)) for k in (1, 2, 3)]
    y_peer = [None] + [(row, turn(y, k) * 4 + x) for k in (1, 2, 3)]

    barrier = pltpu.get_barrier_semaphore()
    partners = plane + z_peer[1:] + other_z[1:] + [twin]
    for peer in partners:
        pl.semaphore_signal(barrier, inc=1, device_id=peer, device_id_type=MESH)
    me = row * 16 + col
    own_rows = pltpu.make_async_copy(own_ref, all_ref.at[pl.ds(me, 1)], local_sem.at[2])
    own_rows.start()
    pl.semaphore_wait(barrier, len(partners))

    sent = []

    def send(src, dst, send_sem, recv_sem, peer, keep=True):
        copy = pltpu.make_async_remote_copy(
            src_ref=src, dst_ref=dst, send_sem=send_sem, recv_sem=recv_sem,
            device_id=peer, device_id_type=MESH,
        )
        copy.start()
        if keep:
            sent.append(copy)
        return copy

    def arrive(ref, sem):
        pltpu.make_async_copy(ref, ref, sem).wait()

    for k in range(1, 16):
        part = all_ref.at[pl.ds(me, 1)]
        send(own_ref, part, block_send.at[k - 1], block_recv.at[k - 1], plane[k - 1])

    half = 256
    step = half // CHUNKS

    def slot(which, holder):
        same = 1 - jnp.abs(which // 2 - holder)
        odd = lax.rem(which, 2)
        return same * (2 * odd + holder) + (1 - same) * (4 + odd)

    holds = y == z
    my_slot = slot(x, core)

    def cross_part(q):
        return cross_ref.at[pl.ds(core * half + q * step, step)]

    def rows_part(s, q):
        return rows_ref.at[s, pl.ds(q * step, step)]

    def y_copy(q, k):
        return pltpu.make_async_remote_copy(
            src_ref=cross_part(q), dst_ref=rows_part(my_slot, q),
            send_sem=cross_send.at[0, q, k - 1], recv_sem=cross_recv.at[0, q],
            device_id=y_peer[k], device_id_type=MESH,
        )

    def own_copy(q):
        return pltpu.make_async_copy(cross_part(q), rows_part(my_slot, q), cross_recv.at[0, q])

    @pl.when(holds)
    def _():
        for q in range(CHUNKS):
            own_copy(q).start()
        for q in range(CHUNKS):
            for k in (1, 3, 2):
                y_copy(q, k).start()

    def pass_x(q):
        arrive(rows_part(my_slot, q), cross_recv.at[0, q])
        for i, k in enumerate((1, 3)):
            send(rows_part(my_slot, q), rows_part(my_slot, q),
                 cross_send.at[1, q, i], cross_recv.at[1 + i, q], x_peer[k])

    def pass_on(q):
        for i, k in enumerate((1, 3)):
            s = slot(turn(x, 4 - k), core)
            arrive(rows_part(s, q), cross_recv.at[1 + i, q])
            piece = rows_ref.at[s, pl.ds(q * step + i * (step // 2), step // 2)]
            send(piece, piece, cross_send.at[2, q, i], cross_recv.at[3 + i, q], x_peer[k])

    def far_x(q):
        s = slot(turn(x, 2), core)
        for i in range(2):
            piece = rows_ref.at[s, pl.ds(q * step + i * (step // 2), step // 2)]
            arrive(piece, cross_recv.at[3 + i, q])

    def twin_rows(part, parts):
        size = half // parts
        for j in range(2):
            send(rows_ref.at[4 + j, pl.ds(part * size, size)],
                 rows_ref.at[2 * j + core, pl.ds(part * size, size)],
                 cross_send.at[3, part, j], cross_recv.at[5 + j, part], twin)

    def twin_rows_arrive(part, parts):
        size = half // parts
        for j in range(2):
            arrive(rows_ref.at[2 * j + 1 - core, pl.ds(part * size, size)],
                   cross_recv.at[5 + j, part])

    def pixel_rows(owner_row, start, count):
        return pixels_ref.at[pl.ds(owner_row * 64 + start, count)]

    def pixels_start():
        local = pltpu.make_async_copy(pixel_ref, pixel_rows(row, 0, 64), local_sem.at[0])
        local.start()
        for q in range(1):
            for i, k in enumerate((1, 3)):
                send(pixel_ref, pixel_rows(row, 0, 64),
                     pixel_send.at[0, q, i], pixel_recv.at[0, q, i], z_peer[k])
        send(pixel_ref, pixel_rows(row, 0, 64), pixel_send.at[2, 0, 0], pixel_recv.at[2, 0, 0], twin)
        return local

    def pixels_on(q):
        for i, k in enumerate((1, 3)):
            owner = turn(z, 4 - k) * 2 + core
            arrive(pixel_rows(owner, 0, 64), pixel_recv.at[0, q, i])
            piece = pixel_rows(owner, 32 * i, 32)
            send(piece, piece, pixel_send.at[1, q, i], pixel_recv.at[1, q, i], z_peer[k])
            whole = pixel_rows(owner, 0, 64)
            send(whole, whole, pixel_send.at[3, q, i], pixel_recv.at[3, q, i], twin)

    def pixels_far(q):
        owner = turn(z, 2) * 2 + core
        for i in range(2):
            piece = pixel_rows(owner, 32 * i, 32)
            arrive(piece, pixel_recv.at[1, q, i])
        whole = pixel_rows(owner, 0, 64)
        send(whole, whole, pixel_send.at[4, q, 0], pixel_recv.at[4, q, 0], twin)

    def pixels_end():
        arrive(pixel_rows(z * 2 + 1 - core, 0, 64), pixel_recv.at[2, 0, 0])
        for q in range(1):
            for i, k in enumerate((1, 3)):
                arrive(pixel_rows(turn(z, 4 - k) * 2 + 1 - core, 0, 64), pixel_recv.at[3, q, i])
            arrive(pixel_rows(turn(z, 2) * 2 + 1 - core, 0, 64), pixel_recv.at[4, q, 0])

    def sector_columns(owner_row):
        return sector_ref.at[:, pl.ds(pl.multiple_of(owner_row * 128, 128), 128)]

    sector_peers = z_peer[1:] + other_z[1:] + [twin]
    peer_rows = [p[0] for p in sector_peers]

    def sectors_start():
        mine = sectors_ref.at[pl.ds(row * 64, 64)]
        local = pltpu.make_async_copy(sector_columns(row), mine, local_sem.at[1])
        local.start()
        for i, peer in enumerate(sector_peers):
            send(sector_columns(peer_rows[i]), mine, sector_send.at[i], sector_recv.at[i], peer)
        return local

    def sectors_end():
        for i in range(7):
            if i == 6:
                source = z * 2 + 1 - core
            else:
                other = (i // 3)
                back = turn(z, 4 - (i % 3 + 1))
                source = back * 2 + (core if other == 0 else 1 - core)
            arrive(sectors_ref.at[pl.ds(source * 64, 64)], sector_recv.at[i])

    for k in range(1, 16):
        source = row * 16 + turn(y, (16 - k) // 4 if k % 4 == 0 else 4 - k // 4) * 4 + turn(x, 4 - k % 4)
        arrive(all_ref.at[pl.ds(source, 1)], block_recv.at[k - 1])

    own_rows.wait()

    def block_part(zs, which):
        return all_ref.at[pl.ds(zs * 32 + which * 16, 16), :, pl.ds(0, 128 * (zs + 1))]

    def block_copies(zs):
        part = block_part(zs, core)
        return [
            pltpu.make_async_remote_copy(
                src_ref=part, dst_ref=part, send_sem=block_send.at[14 + k],
                recv_sem=block_recv.at[15 + zs], device_id=z_peer[k], device_id_type=MESH,
            )
            for k in (1, 2, 3)
        ]

    def block_twin(zs):
        part = block_part(zs, core)
        return pltpu.make_async_remote_copy(
            src_ref=part, dst_ref=part, send_sem=block_send.at[18 + zs],
            recv_sem=block_recv.at[19 + zs], device_id=twin, device_id_type=MESH,
        )

    for zs in range(4):
        @pl.when(z == zs)
        def _(zs=zs):
            for copy in block_copies(zs):
                copy.start()
            block_twin(zs).start()

    local = [pixels_start()]

    def block_relay(zs):
        @pl.when(z != zs)
        def _():
            arrive(block_part(zs, core), block_recv.at[15 + zs])
            block_twin(zs).start()

    def block_ready(zs):
        arrive(block_part(zs, 1 - core), block_recv.at[19 + zs])

    def load_rows(zs):
        width = 128 * (zs + 1)
        for i in range(32):
            m_ref[128 * zs + 4 * i : 128 * zs + 4 * i + 4, :width] = all_ref[32 * zs + i, :, :width]

    for q in range(CHUNKS):
        @pl.when(holds)
        def _(q=q):
            arrive(rows_part(my_slot, q), cross_recv.at[0, q])
            for i, k in enumerate((1, 3)):
                pltpu.make_async_remote_copy(
                    src_ref=rows_part(my_slot, q), dst_ref=rows_part(my_slot, q),
                    send_sem=cross_send.at[1, q, i], recv_sem=cross_recv.at[1 + i, q],
                    device_id=x_peer[k], device_id_type=MESH,
                ).start()

    def pass_x_other(q):
        @pl.when(jnp.logical_not(holds))
        def _():
            arrive(rows_part(my_slot, q), cross_recv.at[0, q])
            for i, k in enumerate((1, 3)):
                pltpu.make_async_remote_copy(
                    src_ref=rows_part(my_slot, q), dst_ref=rows_part(my_slot, q),
                    send_sem=cross_send.at[1, q, i], recv_sem=cross_recv.at[1 + i, q],
                    device_id=x_peer[k], device_id_type=MESH,
                ).start()

    local.append(sectors_start())
    inverse_ref[...] = jnp.zeros_like(inverse_ref)
    block_relay(0)
    pass_x_other(0)
    block_ready(0)
    load_rows(0)

    def rest_of_block():
        for zs in (1, 2, 3):
            block_relay(zs)

    plan = {
        (0, 7): [lambda: pass_x_other(1)],
        (0, 11): [rest_of_block],
        (0, 15): [lambda: [(block_ready(zs), load_rows(zs)) for zs in (1, 2, 3)]],
        (1, 0): [lambda: pass_on(0)],
        (1, 3): [lambda: pass_x_other(2)],
        (1, 8): [lambda: pass_on(1)],
        (1, 14): [lambda: pixels_on(0)],
        (1, 15): [lambda: pass_x_other(3)],
        (2, 4): [lambda: pass_on(2), lambda: far_x(0)],
        (2, 10): [lambda: far_x(1), lambda: twin_rows(0, 2)],
        (2, 15): [lambda: pass_on(3)],
        (3, 4): [lambda: pixels_far(0)],
        (3, 8): [lambda: far_x(2)],
        (3, 12): [lambda: far_x(3), lambda: twin_rows(1, 2)],
    }

    n = inverse_ref.shape[0]
    later = []
    for b in range(n // 128):
        s, e = b * 128, b * 128 + 128
        jobs, later = later, []

        def store(g, value):
            inverse_ref[s + 8 * g : s + 8 * g + 8, s:e] = value

        def after(g):
            if g == 0:
                for job in jobs:
                    job()
            for action in plan.get((b, g), ()):
                action()

        invert_tile(m_ref[s:e, s:e], store, after)

        if e < n:
            below_ref[e:] = dot_nt(m_ref[e:, s:e], inverse_ref[s:e, s:e])
            near = below_ref[e : e + 128]
            m_ref[e : e + 128, e : e + 128] -= dot_nt(near, near)

        def finish_row(s=s, e=e):
            inverse_ref[s:e, :s] = dot_nn(inverse_ref[s:e, s:e], m_ref[s:e, :s])

        def update_rest(s=s, e=e):
            m_ref[e + 128 :, e:] -= dot_nt(below_ref[e + 128 :], below_ref[e:])

        def update_left(s=s, e=e):
            m_ref[e:, :s] -= dot_nn(below_ref[e:], inverse_ref[s:e, :s])

        def update_here(s=s, e=e):
            m_ref[e:, s:e] = -dot_nn(below_ref[e:], inverse_ref[s:e, s:e])

        if b:
            later.append(finish_row)
        if e < n:
            if e + 128 < n:
                later.append(update_rest)
            if b:
                later.append(update_left)
            later.append(update_here)
    for job in later:
        job()

    pixels_end()
    sectors_end()
    for part in range(2):
        twin_rows_arrive(part, 2)
    for copy in local:
        copy.wait()
    for copy in sent:
        copy.wait_send()

    @pl.when(holds)
    def _():
        for q in range(CHUNKS):
            for k in (1, 2, 3):
                y_copy(q, k).wait_send()

    for q in range(CHUNKS):
        for i, k in enumerate((1, 3)):
            part = rows_part(my_slot, q)
            pltpu.make_async_copy(part, part, cross_send.at[1, q, i]).wait()
    for zs in range(4):
        @pl.when(z == zs)
        def _(zs=zs):
            for copy in block_copies(zs):
                copy.wait_send()
        block_twin(zs).wait_send()


def panel(own, cross, pixels, sectors):
    dma = pltpu.SemaphoreType.DMA
    anywhere = pl.BlockSpec(memory_space=pl.ANY)
    return pl.pallas_call(
        panel_kernel,
        out_shape=(
            jax.ShapeDtypeStruct((512, 512), jnp.float32),
            jax.ShapeDtypeStruct((6, 256, 512), jnp.float32),
            jax.ShapeDtypeStruct((512, 2048), jnp.float32),
            jax.ShapeDtypeStruct((512, 128), jnp.float32),
        ),
        in_specs=[anywhere] * 4,
        out_specs=(pl.BlockSpec(memory_space=pltpu.VMEM), anywhere, anywhere, anywhere),
        scratch_shapes=[
            pltpu.VMEM((128, 4, 512), jnp.float32),
            pltpu.VMEM((512, 512), jnp.float32),
            pltpu.VMEM((512, 128), jnp.float32),
            dma((22,)), dma((23,)),
            dma((4, CHUNKS, 3)), dma((7, CHUNKS)),
            dma((5, 2, 2)), dma((5, 2, 2)),
            dma((7,)), dma((7,)),
            dma((3,)),
        ],
        compiler_params=pltpu.CompilerParams(
            collective_id=0, has_side_effects=True, vmem_limit_bytes=16 << 20
        ),
        cost_estimate=pl.CostEstimate(
            flops=40_000_000_000, bytes_accessed=16 << 20, transcendentals=0
        ),
        name="panel",
    )(own, cross, pixels, sectors)


def high_low(value):
    high = value.astype(jnp.bfloat16)
    return high, (value - high.astype(jnp.float32)).astype(jnp.bfloat16)


def left_cat(value, axis=1):
    high, low = high_low(value)
    return jnp.concatenate([high, high, low], axis=axis)


def right_cat(value, axis):
    high, low = high_low(value)
    return jnp.concatenate([high, low, high], axis=axis)


def mxu(a, b, ca, cb):
    return lax.dot_general(a, b, (((ca,), (cb,)), ((), ())), preferred_element_type=jnp.float32)


def product_kernel(
    own_ref, cross_ref, rows_ref, inverse_ref, sectors_ref, trail_sectors_ref,
    trail_ref, pixels_ref, trail_pixels_ref,
    factor_out, columns_out, trail_out, pixels_out, sectors_out, predicted_out,
    rows_cat, columns_cat, coupling_cat, weights_cat,
):
    step = pl.program_id(0)
    device = lax.axis_index("row") * 16 + lax.axis_index("col")

    @pl.when(step == 0)
    def _():
        inverse = inverse_ref[...]
        by_column = right_cat(inverse, 1)
        by_row = right_cat(inverse, 0)
        own = mxu(left_cat(own_ref[...]), by_column, 1, 1)
        lane = lax.broadcasted_iota(jnp.int32, own.shape, 1)
        line = lax.broadcasted_iota(jnp.int32, own.shape, 0) + device * 4
        factor_out[...] = jnp.where(lane <= line, own, 0.0)
        lower = right_cat(inverse[:256, :256], 1)
        last = right_cat(inverse[256:, 256:], 0)

        def times_upper(value):
            high, low = high_low(value)
            near = jnp.concatenate([high[:, :256], high[:, :256], low[:, :256]], axis=1)
            full = jnp.concatenate([high, high, low], axis=1)
            return jnp.concatenate(
                [mxu(near, lower, 1, 1), mxu(full, by_column[256:], 1, 1)], axis=1
            )

        columns = times_upper(cross_ref[...])
        columns_out[...] = columns
        columns_cat[...] = right_cat(columns, 1)
        for i in range(2):
            part = slice(512 * i, 512 * i + 512)
            high, low = high_low(times_upper(rows_ref[2 * i : 2 * i + 2].reshape(512, 512)))
            panel_rows = jnp.concatenate([high, high, low], axis=1)
            rows_cat[part] = panel_rows
            far = jnp.concatenate([high[:, 256:], high[:, 256:], low[:, 256:]], axis=1)
            coupling_cat[part] = left_cat(jnp.concatenate(
                [mxu(panel_rows, by_row[:, :256], 1, 0), mxu(far, last, 1, 0)], axis=1
            ))
        solved = mxu(left_cat(inverse), right_cat(sectors_ref[...], 0), 1, 0)
        solved_cat = right_cat(solved, 0)
        sectors_out[...] = trail_sectors_ref[...] - mxu(left_cat(columns), solved_cat, 1, 0)
        weights = mxu(left_cat(inverse.T), solved_cat, 1, 0)
        weights_cat[...] = left_cat(weights.T)

    width = pixels_out.shape[1]
    part = pl.ds(pl.multiple_of(step * width, width), width)
    tile = right_cat(pixels_ref[:, part], 0)
    pixels_out[...] = trail_pixels_ref[:, part] - mxu(coupling_cat[...], tile, 1, 0)
    predicted_out[...] = mxu(weights_cat[...], tile, 1, 0).T
    size = trail_out.shape[0]
    lines = pl.ds(pl.multiple_of(step * size, size), size)
    trail_out[...] = trail_ref[lines, :] - mxu(rows_cat[lines, :], columns_cat[...], 1, 1)


def products(own, cross, rows, inverse, sectors, trail_sectors, trail, pixels, trail_pixels):
    n, width = pixels.shape
    steps = 4
    height = trail.shape[0]

    def fixed(shape):
        return pl.BlockSpec(shape, lambda i: (0,) * len(shape), pipeline_mode=pl.Buffered(1))

    f32 = lambda *shape: jax.ShapeDtypeStruct(shape, jnp.float32)
    bf16 = lambda *shape: pltpu.VMEM(shape, jnp.bfloat16)
    return pl.pallas_call(
        product_kernel,
        grid=(steps,),
        out_shape=(
            f32(*own.shape), f32(*cross.shape), f32(*trail.shape), f32(*trail_pixels.shape),
            f32(*trail_sectors.shape), f32(width, sectors.shape[1]),
        ),
        in_specs=[pl.BlockSpec(memory_space=pltpu.VMEM)] * 9,
        out_specs=(
            fixed(own.shape), fixed(cross.shape),
            pl.BlockSpec((height // steps, trail.shape[1]), lambda i: (i, 0)),
            pl.BlockSpec((height, width // steps), lambda i: (0, i)),
            fixed(trail_sectors.shape),
            pl.BlockSpec((width // steps, sectors.shape[1]), lambda i: (i, 0)),
        ),
        scratch_shapes=[
            bf16(height, 3 * n), bf16(cross.shape[0], 3 * n), bf16(height, 3 * n),
            bf16(sectors.shape[1], 3 * n),
        ],
        compiler_params=pltpu.CompilerParams(vmem_limit_bytes=26 << 20),
        cost_estimate=pl.CostEstimate(
            flops=13_500_000_000, bytes_accessed=32 << 20, transcendentals=0
        ),
        name="products",
    )(own, cross, rows, inverse, sectors, trail_sectors, trail, pixels, trail_pixels)


def shards(
    panel_block, panel_cross, trail_block, panel_pixels, trail_pixels, panel_sectors, trail_sectors
):
    in_hbm = lambda v: pltpu.with_memory_space_constraint(v, pltpu.HBM)
    inverse, rows, pixels, sectors = panel(
        in_hbm(panel_block.reshape(1, 4, 512)), in_hbm(panel_cross), in_hbm(panel_pixels), in_hbm(panel_sectors)
    )
    return products(
        panel_block, panel_cross, rows, inverse, sectors, trail_sectors, trail_block, pixels, trail_pixels
    )


def solution(mesh):
    return jax.shard_map(
        shards,
        mesh=mesh,
        in_specs=(
            P(("row", "col"), None),
            P("col", None),
            P("row", "col"),
            P("row", "col"),
            P("row", "col"),
            P("row", None),
            P("col", "row"),
        ),
        out_specs=(
            P(("row", "col"), None),
            P("col", None),
            P("row", "col"),
            P("row", "col"),
            P("col", "row"),
            P("col", "row"),
        ),
        check_vma=False,
    )
```
